256 devices in a mesh: blk: 64 (over z_lo, x, y), grp: 4 (over z_hi, core).
Axes of the slice: x: 4, y: 4, z: 8 (z_hi: 2, z_lo: 4; z = z_hi * 4 + z_lo), core: 2. Of those that a mesh axis runs over, the one named last changes fastest.
Arguments:
- source_embed: bfloat16 [131072, 768], P(('blk', 'grp')), may hold values from -60 to 60
- target_embed: bfloat16 [8192, 768], P('blk'), may hold values from -18 to 18
- target_init: float32 [8192], P('blk'), may hold values from -6 to 6
- source_logw: float32 [131072], P(('blk', 'grp')), may hold values from -2 to 2
- target_logw: float32 [8192], P('blk'), may hold values from -2 to 2
Outputs:
- row_pot: float32 [131072], P(('blk', 'grp'))
- column_pot: float32 [8192], P('blk')
The draws below stay inside these ranges and needn't reach their ends.
All inputs are finite; a program needn't handle non-finite values.
Results may differ from the reference program's by a relative error of at most 0.0003.
Values may be sent and summed in bfloat16 or wider, within the bound.
A program may use at most 128 MiB of HBM per device.

```python
import math
import jax
import jax.numpy as jnp
from jax import lax

D = 768
S_DEV = 512
ITERS = 2
S = 131072
NT = 8192


def target_base(key):
    values = jnp.clip(jax.random.normal(jax.random.fold_in(key, 11), (NT, D), jnp.float32), -6.0, 6.0)
    return values


def draw_target_embed(key, part):
    return target_base(key).astype(jnp.bfloat16)


def draw_source_embed(key, part):
    values = jnp.clip(jax.random.normal(jax.random.fold_in(key, 21), (S, D), jnp.float32), -6.0, 6.0)
    return values.astype(jnp.bfloat16)


def steps_of(own_key, dims, pieces, smallest, high):
    level = 1.0
    for axis_at, shards_of in pieces:
        draws = jax.random.uniform(jax.random.fold_in(jax.random.fold_in(own_key, 6), axis_at), (shards_of,), jnp.float32, smallest / len(pieces), high / len(pieces))
        level = level * jnp.repeat(jnp.exp(draws), dims[axis_at] // shards_of).reshape((-1,) + (1,) * (len(dims) - 1 - axis_at))
    return level


def normal_values(rng, dims, width, bound, shards=(), kind=jnp.bfloat16):
    loudness = steps_of(rng, dims, shards, -0.22, 0.18) if shards else 1.0
    values = jax.random.normal(rng, dims, jnp.float32) * width * loudness
    return jnp.minimum(jnp.maximum(values, -bound), bound).astype(kind)


def setup_inputs(seed: int = 0) -> dict:
    key_of = jax.random.split(jax.random.key(seed), 6)
    return {
        "source_embed": draw_source_embed(jax.random.fold_in(key_of[5], 71), 0),
        "target_embed": draw_target_embed(jax.random.fold_in(key_of[5], 71), 0),
        "target_init": normal_values(key_of[2], (NT,), 1.0, 6.0, ((0, 64),), jnp.float32),
        "source_logw": jnp.clip(jax.random.uniform(key_of[3], (S,), jnp.float32, -2.0, 2.0) * steps_of(key_of[3], (S,), ((0, 256),), -0.4, 0.0), -2.0, 2.0),
        "target_logw": jnp.clip(jax.random.uniform(key_of[4], (NT,), jnp.float32, -2.0, 2.0) * steps_of(key_of[4], (NT,), ((0, 64),), -0.4, 0.0), -2.0, 2.0),
    }


epsilon = 0.1
inverse_eps = 10.0

def row_update(cost_matrix, column_pot, row_logw):
    scores = (column_pot[None, :] - cost_matrix) * inverse_eps
    row_top = lax.optimization_barrier(jnp.max(scores, axis=1))
    row_sum = lax.optimization_barrier(jnp.sum(jnp.exp(scores - row_top[:, None]), axis=1))
    return epsilon * row_logw - epsilon * (row_top + jnp.log(row_sum))

def column_partial(cost_matrix, row_pot):
    scores = (row_pot[:, None] - cost_matrix) * inverse_eps
    col_top = lax.optimization_barrier(jnp.max(scores, axis=0))
    col_sum = lax.optimization_barrier(jnp.sum(jnp.exp(scores - col_top[None, :]), axis=0))
    return (col_top, col_sum)

def reference(source_embed, target_embed, target_init, source_logw, target_logw):
    factor = -1.0 / math.sqrt(D)
    slabs = source_embed.reshape(S // S_DEV, S_DEV, D)
    weights = source_logw.reshape(S // S_DEV, S_DEV)

    def half_sweep(column_pot):

        def one_slab(slab_pair):
            slab_rows, slab_logw = slab_pair
            cost_matrix = lax.dot_general(slab_rows, target_embed, (((1,), (1,)), ((), ())), preferred_element_type=jnp.float32) * factor
            row_pot = row_update(cost_matrix, column_pot, slab_logw)
            col_top, col_sum = column_partial(cost_matrix, row_pot)
            return (row_pot, col_top, col_sum)
        row_pot, tops, sums = lax.map(one_slab, (slabs, weights))
        col_peak = lax.optimization_barrier(jnp.max(tops, axis=0))
        col_total = lax.optimization_barrier(jnp.sum(sums * jnp.exp(tops - col_peak[None, :]), axis=0))
        new_column = epsilon * target_logw - epsilon * (col_peak + jnp.log(col_total))
        return (row_pot.reshape(S), new_column)
    column_pot = target_init
    row_pot = jnp.zeros((S,), jnp.float32)
    for iteration in range(ITERS):
        row_pot, column_pot = half_sweep(column_pot)
    return (row_pot, column_pot)
```

```python
import math

import jax
import jax.numpy as jnp
from jax import lax
from jax.experimental import pallas as pl
from jax.experimental.pallas import tpu as pltpu
from jax.sharding import PartitionSpec as P

D = 768
LOG2E = math.log2(math.e)
TO2 = 10.0 * LOG2E
SCALE = TO2 / math.sqrt(D)
NX, NY, NZ = 4, 4, 8
R = 4
MESH = pl.DeviceIdType.MESH
ORDERS = (("x", "y", "z"), ("y", "z", "x"), ("z", "x", "y"))


def lse2(stack):
    top = jnp.max(stack, axis=0)
    return top + jnp.log2(jnp.sum(jnp.exp2(stack - top[None]), axis=0))


def rem4(v):
    return lax.rem(v, 4)


def kernel(
    src_in, tgt_in, init_in, slogw_in, tlogw_in, row_out, col_out,
    src, tgt, aux, cost, grep, gsend, gbuf, mrow, srow, frep, wrow, lrow, lget, frow,
    lsend, abuf, zsend, bbuf, fbuf, hbuf,
    send, recv, loc,
):
    b, g = lax.axis_index("blk"), lax.axis_index("grp")
    core, zh = rem4(g) % 2, lax.div(g, 2)
    zl, x, y = lax.div(b, 16), rem4(lax.div(b, 4)), rem4(b)
    z = zh * 4 + zl
    me = {"x": x, "y": y, "z": zl}

    def dev(px, py, pz, pc):
        return (rem4(pz) * 16 + px * 4 + py, lax.div(pz, 4) * 2 + pc)

    def step(dim, by):
        if dim == "x":
            return dev(rem4(x + by + NX), y, z, core)
        if dim == "y":
            return dev(x, rem4(y + by + NY), z, core)
        return dev(x, y, lax.rem(z + by + NZ, NZ), core)

    partner = dev(x, y, z, 1 - core)
    plane = [(dx, dy, dev(rem4(x + dx), rem4(y + dy), z, core)) for dx in range(4) for dy in range(4)][1:]
    line = [(dz, dev(x, y, lax.rem(z + dz, NZ), core)) for dz in range(1, NZ)]
    across = [(dz, dev(x, y, lax.rem(z + dz, NZ), 1 - core)) for dz in range(NZ)]

    barrier = pltpu.get_barrier_semaphore()
    peers = [p[-1] for p in plane] + [p[-1] for p in line] + [p[-1] for p in across]
    for peer in peers:
        pl.semaphore_signal(barrier, inc=1, device_id=peer, device_id_type=MESH)

    half = pl.multiple_of(core * 64, 64)
    rows_at = pl.multiple_of(core * 512, 512)
    locals_ = [pltpu.make_async_copy(src_in, src.at[pl.ds(rows_at, 512), :], loc.at[3])]
    for t, (d0, d1, d2) in enumerate(ORDERS):
        locals_.append(
            pltpu.make_async_copy(
                tgt_in.at[pl.ds(half, 64), pl.ds(256 * t, 256)],
                tgt.at[t, me[d2], me[d1], me[d0]],
                loc.at[t],
            )
        )
    for copy in locals_:
        copy.start()
    aux[zl, y, x] = jnp.concatenate([init_in[...], tlogw_in[...]], axis=0)
    wrow[core] = slogw_in[...]

    count = [0]
    started = []

    def remote(src_ref, dst_ref, to, slot=None):
        if slot is None:
            slot = count[0]
            count[0] += 1
        return pltpu.make_async_remote_copy(
            src_ref=src_ref, dst_ref=dst_ref, send_sem=send.at[slot], recv_sem=recv.at[slot],
            device_id=to, device_id_type=MESH,
        )

    def go(copy):
        copy.start()
        started.append(copy)

    def drop(copy):
        started[:] = [c for c in started if c is not copy]

    class Ring:
        def __init__(self, dim, unit, low=None, high=None):
            self.dim, self.unit = dim, unit
            self.low, self.high = low or unit, high
            self.base = count[0]
            count[0] += 4
            c = me[dim]
            self.c, self.prev, self.next, self.far = c, rem4(c + 3), rem4(c + 1), rem4(c + 2)

        def begin(self):
            u = self.unit(self.c)
            go(remote(u, u, step(self.dim, 1), self.base))
            go(remote(u, u, step(self.dim, -1), self.base + 1))

        def mid(self):
            u = self.unit(self.prev)
            remote(u, u, step(self.dim, 1), self.base).wait_recv()
            v = self.low(self.prev)
            go(remote(v, v, step(self.dim, 1), self.base + 2))
            u = self.unit(self.next)
            remote(u, u, step(self.dim, -1), self.base + 1).wait_recv()
            if self.high is not None:
                v = self.high(self.next)
                go(remote(v, v, step(self.dim, -1), self.base + 3))

        def end(self):
            v = self.low(self.far)
            remote(v, v, step(self.dim, 1), self.base + 2).wait_recv()
            if self.high is not None:
                v = self.high(self.far)
                remote(v, v, step(self.dim, -1), self.base + 3).wait_recv()

    def rings(t):
        d0, d1, d2 = ORDERS[t]
        c1, c2 = me[d1], me[d2]
        one = Ring(
            d0,
            lambda i: tgt.at[t, c2, c1, i],
            lambda i: tgt.at[t, c2, c1, i, pl.ds(0, 32), :],
            lambda i: tgt.at[t, c2, c1, i, pl.ds(32, 32), :],
        )
        two = Ring(
            d1,
            lambda i: tgt.at[t, c2, i],
            lambda i: tgt.at[t, c2, i, pl.ds(0, 2)],
            lambda i: tgt.at[t, c2, i, pl.ds(2, 2)],
        )
        three = []
        for by in (0, 3, 1, 2):
            r1 = rem4(c1 + by)
            three.append(
                Ring(
                    d2,
                    lambda i, r1=r1: tgt.at[t, i, r1],
                    lambda i, r1=r1: tgt.at[t, i, r1, pl.ds(0, 2)],
                    lambda i, r1=r1: tgt.at[t, i, r1, pl.ds(2, 2)],
                )
            )
        return one, two, three

    all_rings = [rings(t) for t in range(3)]
    aux_rings = [
        Ring("x", lambda i: aux.at[zl, y, i]),
        Ring("y", lambda i: aux.at[zl, i]),
        Ring("z", lambda i: aux.at[i]),
    ]

    for copy in locals_[1:]:
        copy.wait()
    pl.semaphore_wait(barrier, len(peers))

    for one, _, _ in all_rings:
        one.begin()
    aux_rings[0].begin()
    swap_w = remote(wrow.at[core], wrow.at[core], partner)
    go(swap_w)
    locals_[0].wait()
    mine = src.at[pl.ds(rows_at, 512), :]
    swap_src = remote(mine, mine, partner)
    go(swap_src)
    swap_slot = count[0] - 1

    for one, _, _ in all_rings:
        one.mid()
    aux_rings[0].mid()
    for one, two, three in all_rings:
        one.end()
        two.begin()
        three[0].begin()
    aux_rings[0].end()
    aux_rings[1].begin()
    for _, two, three in all_rings:
        two.mid()
        three[1].begin()
        three[2].begin()
    aux_rings[1].mid()
    for _, two, three in all_rings:
        two.end()
        three[3].begin()
    aux_rings[1].end()
    aux_rings[2].begin()

    @pl.loop(0, 16)
    def _(i):
        cost[i] = jnp.zeros((1024, 256), jnp.float32)

    other = src.at[pl.ds(pl.multiple_of(512 - core * 512, 512), 512), :]
    remote(other, other, partner, swap_slot).wait_recv()
    remote(wrow.at[1 - core], wrow.at[1 - core], partner, swap_slot - 1).wait_recv()

    def multiply(t, gx, gy):
        if t == 0:
            rhs = tgt[0, :, gy, gx]
        elif t == 1:
            rhs = tgt[1, gx, :, gy]
        else:
            rhs = tgt[2, gy, gx]
        rhs = rhs.reshape(256, 256)
        cost[gx * 4 + gy] += SCALE * lax.dot_general(
            src[:, 256 * t : 256 * t + 256], rhs, (((1,), (1,)), ((), ())),
            preferred_element_type=jnp.float32,
        )

    @pl.loop(0, 4)
    def _(i):
        multiply(1, x, i)
        multiply(2, i, y)

    for k in range(4):
        for _, _, three in all_rings:
            three[k].mid()
    aux_rings[2].mid()

    @pl.loop(0, 4)
    def _(i):
        for by in (1, 3):
            multiply(1, rem4(x + by), i)
            multiply(2, i, rem4(y + by))

    for k in range(4):
        for _, _, three in all_rings:
            three[k].end()
    aux_rings[2].end()

    @pl.loop(0, 4)
    def _(i):
        multiply(1, rem4(x + 2), i)
        multiply(2, i, rem4(y + 2))

    @pl.loop(0, 16)
    def _(i):
        multiply(0, lax.div(i, 4), rem4(i))

    lanes = lax.broadcasted_iota(jnp.int32, (1, 128), 1)
    low_half = lanes < 64

    def pair(first, second):
        a = jnp.where(low_half, first, pltpu.roll(second, 64, 1))
        c = jnp.where(low_half, pltpu.roll(first, 64, 1), second)
        return jnp.where(core == 0, a, c)

    for gx in range(4):
        for gy in range(4):
            for h in range(2):
                v = pair(aux[2 * h, gy, gx, 0:1, :], aux[2 * h + 1, gy, gx, 0:1, :])
                gbuf[gx * 4 + gy, h : h + 1, :] = v * TO2
    own_w = [
        LOG2E * pair(aux[2 * h, y, x, 1:2, :], aux[2 * h + 1, y, x, 1:2, :]) for h in range(2)
    ]
    own_w = jnp.concatenate(own_w, axis=0)

    eye = lax.broadcasted_iota(jnp.int32, (128, 128), 0) == lax.broadcasted_iota(jnp.int32, (128, 128), 1)

    def row_pass():
        for i in range(16):
            for h in range(2):
                grep[2 * i + h] = jnp.broadcast_to(gbuf[i, h : h + 1, :], (8, 128))

        @pl.loop(0, 128)
        def _(i):
            r = pl.ds(pl.multiple_of(i * 8, 8), 8)
            parts = []
            for j in range(16):
                for h in range(2):
                    parts.append(cost[j, r, 128 * h : 128 * h + 128] + grep[2 * j + h])
            stack = jnp.stack(parts)
            top = jnp.max(stack, axis=0)
            mrow[r, :] = top
            srow[r, :] = jnp.sum(jnp.exp2(stack - top[None]), axis=0)

        for q in range(8):
            r = slice(128 * q, 128 * q + 128)
            m = mrow[r, :]
            top = jnp.max(m, axis=1, keepdims=True)
            total = jnp.sum(srow[r, :] * jnp.exp2(m - top), axis=1, keepdims=True)
            value = jnp.broadcast_to(top + jnp.log2(total), (128, 128))
            lrow[q // 4, q % 4 : q % 4 + 1, :] = jnp.sum(jnp.where(eye, value, 0.0), axis=0, keepdims=True)

    def row_swap(it):
        swap = remote(lrow, lget.at[it], partner)
        go(swap)
        swap.wait_recv()
        swap.wait_send()
        drop(swap)
        a, c = lrow[...], lget[it]
        top = jnp.maximum(a, c)
        both = top + jnp.log2(jnp.exp2(a - top) + jnp.exp2(c - top))
        frow[...] = LOG2E * wrow[...] - both
        for q in range(8):
            line_ = jnp.broadcast_to(frow[q // 4, q % 4 : q % 4 + 1, :], (128, 128))
            col = jnp.sum(jnp.where(eye, line_, 0.0), axis=1, keepdims=True)
            frep[128 * q : 128 * q + 128, :] = jnp.broadcast_to(col, (128, 128))

    def col_pass():
        @pl.loop(0, 16)
        def _(i):
            for h in range(2):
                top = total = None
                for q in range(8):
                    r = slice(128 * q, 128 * q + 128)
                    v = cost[i, r, 128 * h : 128 * h + 128] + frep[r, :]
                    v = v.reshape(16, 8, 128)
                    new = jnp.max(v, axis=0)
                    if top is not None:
                        new = jnp.maximum(top, new)
                    part = jnp.sum(jnp.exp2(v - new[None]), axis=0)
                    total = part if top is None else total * jnp.exp2(top - new) + part
                    top = new
                peak = jnp.max(top, axis=0, keepdims=True)
                mass = jnp.sum(total * jnp.exp2(top - peak), axis=0, keepdims=True)
                lsend[i, h : h + 1, :] = peak + jnp.log2(mass)

    def plane_reduce(it):
        waits = []
        for k, (dx, dy, peer) in enumerate(plane):
            dst = rem4(x + dx) * 4 + rem4(y + dy)
            copy = remote(lsend.at[dst], abuf.at[it, k + 1], peer)
            go(copy)
            waits.append(copy)
        abuf[it, 0] = lsend[x * 4 + y]
        for copy in waits:
            copy.wait_recv()
            copy.wait_send()
            drop(copy)
        return lse2(abuf[it])

    row_pass()
    row_swap(0)
    col_pass()
    zsend[0] = plane_reduce(0)
    waits = []
    for dz, peer in line:
        copy = remote(zsend.at[0], bbuf.at[dz], peer)
        go(copy)
        waits.append(copy)
    bbuf[0] = zsend[0]
    for copy in waits:
        copy.wait_recv()
    gsend[...] = own_w - lse2(bbuf[...])
    gbuf[x * 4 + y] = gsend[...]
    waits = []
    for dx, dy, peer in plane:
        copy = remote(gsend, gbuf.at[x * 4 + y], peer)
        go(copy)
        waits.append((dx, dy, copy, count[0] - 1))
    for dx, dy, copy, slot in waits:
        at = gbuf.at[rem4(x + 4 - dx) * 4 + rem4(y + 4 - dy)]
        remote(at, at, partner, slot).wait_recv()

    row_pass()
    row_swap(1)
    row_out[...] = frow[core] * (1.0 / TO2)
    col_pass()
    zsend[1] = plane_reduce(1)
    waits = []
    for dz, peer in line:
        copy = remote(zsend.at[1], fbuf.at[0, dz], peer)
        go(copy)
        waits.append(copy)
    for dz, peer in across:
        copy = remote(zsend.at[1], fbuf.at[1, dz], peer)
        go(copy)
        waits.append(copy)
    fbuf[0, 0] = zsend[1]
    for copy in waits:
        copy.wait_recv()
    hbuf[core] = lse2(fbuf[0])
    hbuf[1 - core] = lse2(fbuf[1])
    at = pl.ds(lax.div(zl, 2), 1)
    first, second = hbuf[0, at, :], hbuf[1, at, :]
    even = jnp.where(low_half, first, pltpu.roll(second, 64, 1))
    odd = jnp.where(low_half, pltpu.roll(first, 64, 1), second)
    total = jnp.where(rem4(zl) % 2 == 0, even, odd)
    col_out[...] = 0.1 * tlogw_in[...] - (1.0 / TO2) * total

    for copy in started:
        copy.wait_send()


N_SEM = 72 + 12 + 2 + 2 + 30 + 7 + 15 + 15


def shards(source_embed, target_embed, target_init, source_logw, target_logw):
    f32, bf16 = jnp.float32, jnp.bfloat16
    vmem = pl.BlockSpec(memory_space=pltpu.VMEM)
    hbm = pl.BlockSpec(memory_space=pl.ANY)
    row, col = pl.pallas_call(
        kernel,
        out_shape=(jax.ShapeDtypeStruct((4, 128), f32), jax.ShapeDtypeStruct((1, 128), f32)),
        in_specs=[hbm, hbm, vmem, vmem, vmem],
        out_specs=(vmem, vmem),
        scratch_shapes=[
            pltpu.VMEM((1024, D), bf16),
            pltpu.VMEM((3, R, R, R, 64, 256), bf16),
            pltpu.VMEM((R, R, R, 2, 128), f32),
            pltpu.VMEM((16, 1024, 256), f32),
            pltpu.VMEM((32, 8, 128), f32),
            pltpu.VMEM((2, 128), f32),
            pltpu.VMEM((16, 2, 128), f32),
            pltpu.VMEM((1024, 128), f32),
            pltpu.VMEM((1024, 128), f32),
            pltpu.VMEM((1024, 128), f32),
            pltpu.VMEM((2, 4, 128), f32),
            pltpu.VMEM((2, 4, 128), f32),
            pltpu.VMEM((2, 2, 4, 128), f32),
            pltpu.VMEM((2, 4, 128), f32),
            pltpu.VMEM((16, 2, 128), f32),
            pltpu.VMEM((2, 16, 2, 128), f32),
            pltpu.VMEM((2, 2, 128), f32),
            pltpu.VMEM((8, 2, 128), f32),
            pltpu.VMEM((2, 8, 2, 128), f32),
            pltpu.VMEM((2, 2, 128), f32),
            pltpu.SemaphoreType.DMA((N_SEM,)),
            pltpu.SemaphoreType.DMA((N_SEM,)),
            pltpu.SemaphoreType.DMA((4,)),
        ],
        compiler_params=pltpu.CompilerParams(
            collective_id=0, has_side_effects=True, vmem_limit_bytes=60 * 2**20
        ),
    )(
        source_embed, target_embed, target_init.reshape(1, 128),
        source_logw.reshape(4, 128), target_logw.reshape(1, 128),
    )
    return row.reshape(512), col.reshape(128)


def solution(mesh):
    in_specs = (P(("blk", "grp"), None), P("blk", None), P("blk"), P(("blk", "grp")), P("blk"))
    out_specs = (P(("blk", "grp")), P("blk"))
    return jax.shard_map(shards, mesh=mesh, in_specs=in_specs, out_specs=out_specs, check_vma=False)
```

```python
import math

import jax
import jax.numpy as jnp
from jax import lax
from jax.experimental import pallas as pl
from jax.experimental.pallas import tpu as pltpu
from jax.sharding import PartitionSpec as P

D = 768
LOG2E = math.log2(math.e)
TO2 = 10.0 * LOG2E
SCALE = TO2 / math.sqrt(D)
NX, NY, NZ = 4, 4, 8
R = 4
MESH = pl.DeviceIdType.MESH
FAR_FIRST = (2, 1, 3, 0)
ORDERS = (("x", "y", "z"), ("y", "z", "x"), ("z", "x", "y"))


def lse2(stack):
    top = jnp.max(stack, axis=0)
    return top + jnp.log2(jnp.sum(jnp.exp2(stack - top[None]), axis=0))


def rem4(v):
    return lax.rem(v, 4)


def kernel(
    src_in, tgt_in, init_in, slogw_in, tlogw_in, row_out, col_out,
    src, tgt, aux, cost, grep, gsend, gbuf, mrow, srow, frep, wrow, lrow, lget, frow,
    lsend, abuf, zsend, bbuf, fbuf, hbuf,
    send, recv, loc, token,
):
    b, g = lax.axis_index("blk"), lax.axis_index("grp")
    core, zh = rem4(g) % 2, lax.div(g, 2)
    zl, x, y = lax.div(b, 16), rem4(lax.div(b, 4)), rem4(b)
    z = zh * 4 + zl
    me = {"x": x, "y": y, "z": zl}

    def dev(px, py, pz, pc):
        return (rem4(pz) * 16 + px * 4 + py, lax.div(pz, 4) * 2 + pc)

    def step(dim, by):
        if dim == "x":
            return dev(rem4(x + by + NX), y, z, core)
        if dim == "y":
            return dev(x, rem4(y + by + NY), z, core)
        return dev(x, y, lax.rem(z + by + NZ, NZ), core)

    partner = dev(x, y, z, 1 - core)
    plane = [(dx, dy, dev(rem4(x + dx), rem4(y + dy), z, core)) for dx in FAR_FIRST for dy in FAR_FIRST][:15]
    line = [(dz, dev(x, y, lax.rem(z + dz, NZ), core)) for dz in range(1, NZ)]
    across = [(dz, dev(x, y, lax.rem(z + dz, NZ), 1 - core)) for dz in range(NZ)]

    barrier = pltpu.get_barrier_semaphore()
    peers = [step(d, by) for d in ("x", "y", "z") for by in (1, -1)] + [partner]
    for peer in peers:
        pl.semaphore_signal(barrier, inc=1, device_id=peer, device_id_type=MESH)

    half = pl.multiple_of(core * 64, 64)
    rows_at = pl.multiple_of(core * 512, 512)
    locals_ = [pltpu.make_async_copy(src_in, src.at[pl.ds(rows_at, 512), :], loc.at[3])]
    for t, (d0, d1, d2) in enumerate(ORDERS):
        locals_.append(
            pltpu.make_async_copy(
                tgt_in.at[pl.ds(half, 64), pl.ds(256 * t, 256)],
                tgt.at[t, me[d2], me[d1], me[d0]],
                loc.at[t],
            )
        )
    for copy in locals_:
        copy.start()
    aux[zl, y, x] = jnp.concatenate([init_in[...], tlogw_in[...]], axis=0)
    wrow[core] = slogw_in[...]

    count = [0]
    started = []

    def remote(src_ref, dst_ref, to, slot=None):
        if slot is None:
            slot = count[0]
            count[0] += 1
        return pltpu.make_async_remote_copy(
            src_ref=src_ref, dst_ref=dst_ref, send_sem=send.at[slot], recv_sem=recv.at[slot],
            device_id=to, device_id_type=MESH,
        )

    def go(copy):
        copy.start()
        started.append(copy)

    def drop(copy):
        started[:] = [c for c in started if c is not copy]

    class Ring:
        def __init__(self, dim, unit, low=None, high=None):
            self.dim, self.unit = dim, unit
            self.low, self.high = low or unit, high
            self.base = count[0]
            count[0] += 4
            c = me[dim]
            self.c, self.prev, self.next, self.far = c, rem4(c + 3), rem4(c + 1), rem4(c + 2)

        def begin(self):
            u = self.unit(self.c)
            go(remote(u, u, step(self.dim, 1), self.base))
            go(remote(u, u, step(self.dim, -1), self.base + 1))

        def mid(self):
            u = self.unit(self.prev)
            remote(u, u, step(self.dim, 1), self.base).wait_recv()
            v = self.low(self.prev)
            go(remote(v, v, step(self.dim, 1), self.base + 2))
            u = self.unit(self.next)
            remote(u, u, step(self.dim, -1), self.base + 1).wait_recv()
            if self.high is not None:
                v = self.high(self.next)
                go(remote(v, v, step(self.dim, -1), self.base + 3))

        def end(self):
            v = self.low(self.far)
            remote(v, v, step(self.dim, 1), self.base + 2).wait_recv()
            if self.high is not None:
                v = self.high(self.far)
                remote(v, v, step(self.dim, -1), self.base + 3).wait_recv()

    def rings(t):
        d0, d1, d2 = ORDERS[t]
        c1, c2 = me[d1], me[d2]
        one = Ring(
            d0,
            lambda i: tgt.at[t, c2, c1, i],
            lambda i: tgt.at[t, c2, c1, i, pl.ds(0, 32), :],
            lambda i: tgt.at[t, c2, c1, i, pl.ds(32, 32), :],
        )
        two = Ring(
            d1,
            lambda i: tgt.at[t, c2, i],
            lambda i: tgt.at[t, c2, i, pl.ds(0, 2)],
            lambda i: tgt.at[t, c2, i, pl.ds(2, 2)],
        )
        three = []
        for by in (0, 3, 1, 2):
            r1 = rem4(c1 + by)
            three.append(
                Ring(
                    d2,
                    lambda i, r1=r1: tgt.at[t, i, r1],
                    lambda i, r1=r1: tgt.at[t, i, r1, pl.ds(0, 2)],
                    lambda i, r1=r1: tgt.at[t, i, r1, pl.ds(2, 2)],
                )
            )
        return one, two, three

    all_rings = [rings(t) for t in range(3)]
    aux_rings = [
        Ring("x", lambda i: aux.at[zl, y, i]),
        Ring("y", lambda i: aux.at[zl, i]),
        Ring("z", lambda i: aux.at[i]),
    ]

    for copy in locals_[1:]:
        copy.wait()
    pl.semaphore_wait(barrier, len(peers))

    for one, _, _ in all_rings:
        one.begin()
    aux_rings[0].begin()
    swap_w = remote(wrow.at[core], wrow.at[core], partner)
    go(swap_w)
    locals_[0].wait()
    mine = src.at[pl.ds(rows_at, 512), :]
    swap_src = remote(mine, mine, partner)
    go(swap_src)
    swap_slot = count[0] - 1

    for one, _, _ in all_rings:
        one.mid()
    aux_rings[0].mid()
    for one, two, three in all_rings:
        one.end()
        two.begin()
        three[0].begin()
    aux_rings[0].end()
    aux_rings[1].begin()
    for _, two, three in all_rings:
        two.mid()
        three[1].begin()
        three[2].begin()
    aux_rings[1].mid()
    for _, two, three in all_rings:
        two.end()
        three[3].begin()
    aux_rings[1].end()
    aux_rings[2].begin()

    @pl.loop(0, 16)
    def _(i):
        cost[i] = jnp.zeros((1024, 256), jnp.float32)

    other = src.at[pl.ds(pl.multiple_of(512 - core * 512, 512), 512), :]
    remote(other, other, partner, swap_slot).wait_recv()
    remote(wrow.at[1 - core], wrow.at[1 - core], partner, swap_slot - 1).wait_recv()

    def multiply(t, gx, gy):
        if t == 0:
            rhs = tgt[0, :, gy, gx]
        elif t == 1:
            rhs = tgt[1, gx, :, gy]
        else:
            rhs = tgt[2, gy, gx]
        rhs = rhs.reshape(256, 256)
        cost[gx * 4 + gy] += SCALE * lax.dot_general(
            src[:, 256 * t : 256 * t + 256], rhs, (((1,), (1,)), ((), ())),
            preferred_element_type=jnp.float32,
        )

    @pl.loop(0, 4)
    def _(i):
        multiply(1, x, i)
        multiply(2, i, y)

    for k in range(4):
        for _, _, three in all_rings:
            three[k].mid()
    aux_rings[2].mid()

    @pl.loop(0, 4)
    def _(i):
        for by in (1, 3):
            multiply(1, rem4(x + by), i)
            multiply(2, i, rem4(y + by))

    for k in range(4):
        for _, _, three in all_rings:
            three[k].end()
    aux_rings[2].end()
    for by in (2, -2):
        pl.semaphore_signal(token, inc=1, device_id=step("z", by), device_id_type=MESH)

    @pl.loop(0, 4)
    def _(i):
        multiply(1, rem4(x + 2), i)
        multiply(2, i, rem4(y + 2))

    @pl.loop(0, 16)
    def _(i):
        multiply(0, lax.div(i, 4), rem4(i))

    lanes = lax.broadcasted_iota(jnp.int32, (1, 128), 1)
    low_half = lanes < 64

    def pair(first, second):
        a = jnp.where(low_half, first, pltpu.roll(second, 64, 1))
        c = jnp.where(low_half, pltpu.roll(first, 64, 1), second)
        return jnp.where(core == 0, a, c)

    for gx in range(4):
        for gy in range(4):
            for h in range(2):
                v = pair(aux[2 * h, gy, gx, 0:1, :], aux[2 * h + 1, gy, gx, 0:1, :])
                gbuf[gx * 4 + gy, h : h + 1, :] = v * TO2
    own_w = [
        LOG2E * pair(aux[2 * h, y, x, 1:2, :], aux[2 * h + 1, y, x, 1:2, :]) for h in range(2)
    ]
    own_w = jnp.concatenate(own_w, axis=0)

    eye = lax.broadcasted_iota(jnp.int32, (128, 128), 0) == lax.broadcasted_iota(jnp.int32, (128, 128), 1)

    def row_pass():
        for i in range(16):
            for h in range(2):
                grep[2 * i + h] = jnp.broadcast_to(gbuf[i, h : h + 1, :], (8, 128))

        @pl.loop(0, 128, unroll=4)
        def _(i):
            r = pl.ds(pl.multiple_of(i * 8, 8), 8)
            parts = []
            for j in range(16):
                for h in range(2):
                    parts.append(cost[j, r, 128 * h : 128 * h + 128] + grep[2 * j + h])
            stack = jnp.stack(parts)
            top = jnp.max(stack, axis=0)
            mrow[r, :] = top
            srow[r, :] = jnp.sum(jnp.exp2(stack - top[None]), axis=0)

        for q in range(8):
            r = slice(128 * q, 128 * q + 128)
            m = mrow[r, :].T
            top = jnp.max(m, axis=0, keepdims=True)
            total = jnp.sum(srow[r, :].T * jnp.exp2(m - top), axis=0, keepdims=True)
            lrow[q // 4, q % 4 : q % 4 + 1, :] = top + jnp.log2(total)

    def row_swap(it):
        swap = remote(lrow, lget.at[it], partner)
        go(swap)
        swap.wait_recv()
        swap.wait_send()
        drop(swap)
        a, c = lrow[...], lget[it]
        top = jnp.maximum(a, c)
        both = top + jnp.log2(jnp.exp2(a - top) + jnp.exp2(c - top))
        frow[...] = LOG2E * wrow[...] - both
        for q in range(8):
            line_ = jnp.broadcast_to(frow[q // 4, q % 4 : q % 4 + 1, :], (128, 128))
            col = jnp.sum(jnp.where(eye, line_, 0.0), axis=1, keepdims=True)
            frep[128 * q : 128 * q + 128, :] = jnp.broadcast_to(col, (128, 128))

    def far_first(i):
        return jnp.where(i == 0, 2, jnp.where(i == 1, 1, jnp.where(i == 2, 3, 0)))

    def col_reduce(it):
        base = count[0]
        count[0] += 15

        def owner(i):
            return rem4(x + far_first(lax.div(i, 4))), rem4(y + far_first(rem4(i)))

        def give(i):
            px, py = owner(i)
            return remote(lsend.at[px * 4 + py], abuf.at[it, i], dev(px, py, z, core), base + i)

        @pl.loop(0, 16)
        def _(i):
            px, py = owner(i)
            at = px * 4 + py
            for h in range(2):
                top = total = None
                for q in range(8):
                    r = slice(128 * q, 128 * q + 128)
                    v = cost[at, r, 128 * h : 128 * h + 128] + frep[r, :]
                    v = v.reshape(16, 8, 128)
                    new = jnp.max(v, axis=0)
                    if top is not None:
                        new = jnp.maximum(top, new)
                    part = jnp.sum(jnp.exp2(v - new[None]), axis=0)
                    total = part if top is None else total * jnp.exp2(top - new) + part
                    top = new
                peak = jnp.max(top, axis=0, keepdims=True)
                mass = jnp.sum(total * jnp.exp2(top - peak), axis=0, keepdims=True)
                lsend[at, h : h + 1, :] = peak + jnp.log2(mass)

            @pl.when(i > 0)
            def _():
                give(i - 1).start()

        abuf[it, 15] = lsend[x * 4 + y]

        @pl.loop(0, 15)
        def _(i):
            copy = give(i)
            copy.wait_recv()
            copy.wait_send()

        return lse2(abuf[it])

    row_pass()
    row_swap(0)
    zsend[0] = col_reduce(0)
    pl.semaphore_wait(token, 2)
    waits = []
    for dz, peer in line:
        copy = remote(zsend.at[0], bbuf.at[dz], peer)
        go(copy)
        waits.append(copy)
    bbuf[0] = zsend[0]
    for copy in waits:
        copy.wait_recv()
    gsend[...] = own_w - lse2(bbuf[...])
    gbuf[x * 4 + y] = gsend[...]
    waits = []
    for dx, dy, peer in plane:
        copy = remote(gsend, gbuf.at[x * 4 + y], peer)
        go(copy)
        waits.append((dx, dy, copy, count[0] - 1))
    for dx, dy, copy, slot in waits:
        at = gbuf.at[rem4(x + 4 - dx) * 4 + rem4(y + 4 - dy)]
        remote(at, at, partner, slot).wait_recv()

    row_pass()
    row_swap(1)
    row_out[...] = frow[core] * (1.0 / TO2)
    zsend[1] = col_reduce(1)
    waits = []
    for dz, peer in line:
        copy = remote(zsend.at[1], fbuf.at[0, dz], peer)
        go(copy)
        waits.append(copy)
    for dz, peer in across:
        copy = remote(zsend.at[1], fbuf.at[1, dz], peer)
        go(copy)
        waits.append(copy)
    fbuf[0, 0] = zsend[1]
    for copy in waits:
        copy.wait_recv()
    hbuf[core] = lse2(fbuf[0])
    hbuf[1 - core] = lse2(fbuf[1])
    at = pl.ds(lax.div(zl, 2), 1)
    first, second = hbuf[0, at, :], hbuf[1, at, :]
    even = jnp.where(low_half, first, pltpu.roll(second, 64, 1))
    odd = jnp.where(low_half, pltpu.roll(first, 64, 1), second)
    total = jnp.where(rem4(zl) % 2 == 0, even, odd)
    col_out[...] = 0.1 * tlogw_in[...] - (1.0 / TO2) * total

    for copy in started:
        copy.wait_send()


N_SEM = 72 + 12 + 2 + 2 + 30 + 7 + 15 + 15


def shards(source_embed, target_embed, target_init, source_logw, target_logw):
    f32, bf16 = jnp.float32, jnp.bfloat16
    vmem = pl.BlockSpec(memory_space=pltpu.VMEM)
    hbm = pl.BlockSpec(memory_space=pl.ANY)
    row, col = pl.pallas_call(
        kernel,
        out_shape=(jax.ShapeDtypeStruct((4, 128), f32), jax.ShapeDtypeStruct((1, 128), f32)),
        in_specs=[hbm, hbm, vmem, vmem, vmem],
        out_specs=(vmem, vmem),
        scratch_shapes=[
            pltpu.VMEM((1024, D), bf16),
            pltpu.VMEM((3, R, R, R, 64, 256), bf16),
            pltpu.VMEM((R, R, R, 2, 128), f32),
            pltpu.VMEM((16, 1024, 256), f32),
            pltpu.VMEM((32, 8, 128), f32),
            pltpu.VMEM((2, 128), f32),
            pltpu.VMEM((16, 2, 128), f32),
            pltpu.VMEM((1024, 128), f32),
            pltpu.VMEM((1024, 128), f32),
            pltpu.VMEM((1024, 128), f32),
            pltpu.VMEM((2, 4, 128), f32),
            pltpu.VMEM((2, 4, 128), f32),
            pltpu.VMEM((2, 2, 4, 128), f32),
            pltpu.VMEM((2, 4, 128), f32),
            pltpu.VMEM((16, 2, 128), f32),
            pltpu.VMEM((2, 16, 2, 128), f32),
            pltpu.VMEM((2, 2, 128), f32),
            pltpu.VMEM((8, 2, 128), f32),
            pltpu.VMEM((2, 8, 2, 128), f32),
            pltpu.VMEM((2, 2, 128), f32),
            pltpu.SemaphoreType.DMA((N_SEM,)),
            pltpu.SemaphoreType.DMA((N_SEM,)),
            pltpu.SemaphoreType.DMA((4,)),
            pltpu.SemaphoreType.REGULAR,
        ],
        compiler_params=pltpu.CompilerParams(
            collective_id=0, has_side_effects=True, vmem_limit_bytes=60 * 2**20
        ),
    )(
        source_embed, target_embed, target_init.reshape(1, 128),
        source_logw.reshape(4, 128), target_logw.reshape(1, 128),
    )
    return row.reshape(512), col.reshape(128)


def solution(mesh):
    in_specs = (P(("blk", "grp"), None), P("blk", None), P("blk"), P(("blk", "grp")), P("blk"))
    out_specs = (P(("blk", "grp")), P("blk"))
    return jax.shard_map(shards, mesh=mesh, in_specs=in_specs, out_specs=out_specs, check_vma=False)
```

```python
import math

import jax
import jax.numpy as jnp
from jax import lax
from jax.experimental import pallas as pl
from jax.experimental.pallas import tpu as pltpu
from jax.sharding import PartitionSpec as P

D = 768
LOG2E = math.log2(math.e)
TO2 = 10.0 * LOG2E
SCALE = TO2 / math.sqrt(D)
NZ = 8
R = 4
MESH = pl.DeviceIdType.MESH


def lse2(stack):
    top = jnp.max(stack, axis=0)
    return top + jnp.log2(jnp.sum(jnp.exp2(stack - top[None]), axis=0))


def rem4(v):
    return lax.rem(v, 4)


def kernel(
    src_in, tgt_in, init_in, slogw_in, tlogw_in, row_out, col_out,
    src, buf_a, buf_b, buf_c, aux, cost, grep, gsend, gbuf, mrow, srow, frep, wrow, lrow, lget, frow,
    ltile, lsend, abuf, zsend, bbuf, fbuf, hbuf,
    send, recv, loc, token,
):
    b, g = lax.axis_index("blk"), lax.axis_index("grp")
    core, zh = lax.rem(g, 2), lax.div(g, 2)
    zl, x, y = lax.div(b, 16), rem4(lax.div(b, 4)), rem4(b)
    z = zh * 4 + zl
    u, v = jnp.where(core == 0, x, y), jnp.where(core == 0, y, x)

    def at(du, dv, dz, pc):
        pu, pv, pz = rem4(u + du + 4), rem4(v + dv + 4), lax.rem(z + dz + NZ, NZ)
        px, py = jnp.where(core == 0, pu, pv), jnp.where(core == 0, pv, pu)
        return (rem4(pz) * 16 + px * 4 + py, lax.div(pz, 4) * 2 + pc)

    def step(dim, by):
        return at(by if dim == "u" else 0, by if dim == "v" else 0, by if dim == "z" else 0, core)

    partner = at(0, 0, 0, 1 - core)
    line = [(dz, at(0, 0, dz, core)) for dz in range(1, NZ)]
    across = [(dz, at(0, 0, dz, 1 - core)) for dz in range(NZ)]

    barrier = pltpu.get_barrier_semaphore()
    peers = [step(d, by) for d in ("u", "v", "z") for by in (1, -1)] + [partner]
    for peer in peers:
        pl.semaphore_signal(barrier, inc=1, device_id=peer, device_id_type=MESH)

    half = pl.multiple_of(core * 64, 64)
    rows_at = pl.multiple_of(core * 512, 512)
    locals_ = [
        pltpu.make_async_copy(tgt_in.at[pl.ds(half, 32), :], buf_a.at[0, 0, 0], loc.at[0]),
        pltpu.make_async_copy(tgt_in.at[pl.ds(half + 32, 16), :], buf_b.at[0, 0, 0], loc.at[1]),
        pltpu.make_async_copy(tgt_in.at[pl.ds(half + 48, 16), :], buf_c.at[0, 0, 0], loc.at[2]),
        pltpu.make_async_copy(src_in, src.at[pl.ds(rows_at, 512), :], loc.at[3]),
    ]
    for copy in locals_:
        copy.start()
    aux[0, 0, 0] = jnp.concatenate([init_in[...], tlogw_in[...]], axis=0)
    wrow[core] = slogw_in[...]

    count = [0]
    started = []

    def remote(src_ref, dst_ref, to, slot=None):
        if slot is None:
            slot = count[0]
            count[0] += 1
        return pltpu.make_async_remote_copy(
            src_ref=src_ref, dst_ref=dst_ref, send_sem=send.at[slot], recv_sem=recv.at[slot],
            device_id=to, device_id_type=MESH,
        )

    def go(copy):
        copy.start()
        started.append(copy)

    def drop(copy):
        started[:] = [c for c in started if c is not copy]

    class Ring:
        def __init__(self, dim, unit, low=None, high=None):
            self.dim, self.unit = dim, unit
            self.low, self.high = low or unit, high
            self.base = count[0]
            count[0] += 4
            self.up, self.down = step(dim, 1), step(dim, -1)

        def begin(self):
            go(remote(self.unit(0), self.unit(1), self.up, self.base))
            go(remote(self.unit(0), self.unit(2), self.down, self.base + 1))

        def mid(self):
            remote(self.unit(1), self.unit(1), self.up, self.base).wait_recv()
            go(remote(self.low(1), self.low(3), self.up, self.base + 2))
            remote(self.unit(2), self.unit(2), self.down, self.base + 1).wait_recv()
            if self.high is not None:
                go(remote(self.high(2), self.high(3), self.down, self.base + 3))

        def end(self):
            remote(self.low(3), self.low(3), self.up, self.base + 2).wait_recv()
            if self.high is not None:
                remote(self.high(3), self.high(3), self.down, self.base + 3).wait_recv()

    left, right = pl.ds(0, 384), pl.ds(384, 384)
    every = slice(None)

    class Tree:
        def __init__(self, buf, dims):
            d0, d1, d2 = dims
            self.one = Ring(
                d0, lambda p: buf.at[0, 0, p],
                lambda p: buf.at[0, 0, p, every, left], lambda p: buf.at[0, 0, p, every, right],
            )

            def single(dim, place):
                return Ring(
                    dim, lambda p: buf.at[place(p)],
                    lambda p: buf.at[place(p) + (every, left)], lambda p: buf.at[place(p) + (every, right)],
                )

            both = pl.ds(1, 2)
            self.two = [
                single(d1, lambda p: (0, p, 0)),
                Ring(d1, lambda p: buf.at[0, p, both], lambda p: buf.at[0, p, 1], lambda p: buf.at[0, p, 2]),
                single(d1, lambda p: (0, p, 3)),
            ]
            self.own = [
                single(d2, lambda p: (p, 0, 0)),
                Ring(d2, lambda p: buf.at[p, 0, both], lambda p: buf.at[p, 0, 1], lambda p: buf.at[p, 0, 2]),
                single(d2, lambda p: (p, 0, 3)),
            ]
            self.near = [
                Ring(d2, lambda p, k=k: buf.at[p, both, k], lambda p, k=k: buf.at[p, 1, k], lambda p, k=k: buf.at[p, 2, k])
                for k in (0, both, 3)
            ]
            self.far = Ring(
                d2, lambda p: buf.at[p, 3], lambda p: buf.at[p, 3, pl.ds(0, 2)], lambda p: buf.at[p, 3, pl.ds(2, 2)]
            )

    trees = [Tree(buf_a, ("v", "z", "u")), Tree(buf_b, ("u", "z", "v")), Tree(buf_c, ("u", "v", "z"))]
    aux_rings = [
        Ring("u", lambda p: aux.at[0, 0, p]),
        Ring("v", lambda p: aux.at[0, p]),
        Ring("z", lambda p: aux.at[p]),
    ]

    for copy in locals_[:3]:
        copy.wait()
    pl.semaphore_wait(barrier, len(peers))

    trees[0].one.begin()
    trees[1].one.begin()
    trees[2].one.begin()
    aux_rings[0].begin()
    trees[0].two[0].begin()
    trees[1].two[0].begin()
    trees[2].two[0].begin()
    trees[0].own[0].begin()
    trees[1].own[0].begin()
    trees[2].own[0].begin()
    swap_slot = count[0]
    go(remote(wrow.at[core], wrow.at[core], partner))
    locals_[3].wait()
    mine = src.at[pl.ds(rows_at, 512), :]
    go(remote(mine, mine, partner))
    trees[0].one.mid()
    trees[0].two[1].begin()
    trees[0].own[1].begin()
    trees[1].one.mid()
    trees[1].two[1].begin()
    trees[1].own[1].begin()
    trees[2].one.mid()
    trees[2].two[1].begin()
    aux_rings[0].mid()
    trees[0].two[0].mid()
    trees[0].near[0].begin()
    trees[1].two[0].mid()
    trees[1].near[0].begin()
    trees[2].two[0].mid()
    trees[2].near[0].begin()
    trees[0].one.end()
    trees[0].two[2].begin()
    trees[0].own[2].begin()
    trees[1].one.end()
    trees[1].two[2].begin()
    trees[1].own[2].begin()
    trees[2].one.end()
    trees[2].two[2].begin()
    aux_rings[0].end()
    aux_rings[1].begin()
    trees[2].own[1].begin()
    trees[0].two[1].mid()
    trees[0].near[1].begin()
    trees[1].two[1].mid()
    trees[1].near[1].begin()
    trees[2].two[1].mid()
    trees[2].near[1].begin()
    aux_rings[1].mid()
    trees[0].two[2].mid()
    trees[0].near[2].begin()
    trees[1].two[2].mid()
    trees[1].near[2].begin()
    trees[2].two[2].mid()
    trees[2].near[2].begin()
    trees[2].own[2].begin()
    aux_rings[1].end()
    aux_rings[2].begin()
    trees[0].own[0].mid()
    trees[1].own[0].mid()
    trees[2].own[0].mid()
    trees[0].two[0].end()
    trees[0].two[1].end()
    trees[0].two[2].end()
    trees[0].far.begin()
    trees[1].two[0].end()
    trees[1].two[1].end()
    trees[1].two[2].end()
    trees[1].far.begin()
    trees[2].two[0].end()
    trees[2].two[1].end()
    trees[2].two[2].end()
    trees[2].far.begin()
    trees[0].own[1].mid()
    trees[1].own[1].mid()
    trees[2].own[1].mid()
    trees[0].own[2].mid()
    trees[1].own[2].mid()
    trees[2].own[2].mid()
    aux_rings[2].mid()

    other = src.at[pl.ds(pl.multiple_of(512 - core * 512, 512), 512), :]
    remote(wrow.at[1 - core], wrow.at[1 - core], partner, swap_slot).wait_recv()
    remote(other, other, partner, swap_slot + 1).wait_recv()

    zplace = []
    for k in range(4):
        r = rem4(k - zl + 4)
        zplace.append(jnp.where(r == 0, 0, jnp.where(r == 3, 1, jnp.where(r == 1, 2, 3))))

    def multiply(pieces, tile):
        rhs = jnp.concatenate(pieces, axis=0)
        out = SCALE * lax.dot_general(
            src[...], rhs, (((1,), (1,)), ((), ())), preferred_element_type=jnp.float32
        )
        cost[tile] = out[:, :128]
        cost[tile + 1] = out[:, 128:]

    def multiply_a(pu, pair):
        multiply([buf_a[pu, zp, pair * 2 + k] for k in range(2) for zp in zplace], pu * 4 + pair * 2)

    def multiply_b(pv):
        multiply([buf_b[pv, zp, pu] for pu in range(4) for zp in zplace], 16 + pv * 2)

    def multiply_c(pv):
        multiply([buf_c[zp, pv, pu] for pu in range(4) for zp in zplace], 24 + pv * 2)

    trees[0].near[0].mid()
    trees[1].near[0].mid()
    trees[2].near[0].mid()

    multiply_a(0, 0)
    trees[0].near[1].mid()
    trees[1].near[1].mid()
    trees[2].near[1].mid()

    multiply_a(0, 1)
    trees[0].near[2].mid()
    trees[1].near[2].mid()
    trees[2].near[2].mid()

    multiply_b(0)
    trees[0].far.mid()
    trees[1].far.mid()
    trees[2].far.mid()
    aux_rings[2].end()

    @pl.loop(0, 4)
    def _(i):
        multiply_a(1 + lax.div(i, 2), lax.rem(i, 2))

    @pl.loop(1, 3)
    def _(i):
        multiply_b(i)

    lanes = lax.broadcasted_iota(jnp.int32, (1, 128), 1)
    low_half = lanes < 64
    z_of_first = lax.div(lanes, 32)
    z_of_second = lax.div(lax.rem(lanes, 64), 16)

    def group_of(blocks):
        first = second = jnp.zeros((1, 128), jnp.float32)
        for k, block in enumerate(blocks):
            w = jnp.where(core == 0, block, pltpu.roll(block, 64, 1))
            first = jnp.where(z_of_first == k, pltpu.roll(w, (k * 32) % 128, 1), first)
            w_low = pltpu.roll(w, (k * 16 - 32) % 128, 1)
            w_high = pltpu.roll(w, (k * 16 + 16) % 128, 1)
            second = jnp.where(z_of_second == k, jnp.where(low_half, w_low, w_high), second)
        return jnp.concatenate([first, second], axis=0)

    for pu in range(4):
        for pv in range(4):
            gbuf[pu * 4 + pv] = TO2 * group_of([aux[zp, pv, pu, 0:1, :] for zp in zplace])
    own_w = LOG2E * group_of([aux[zp, 0, 0, 1:2, :] for zp in zplace])

    eye = lax.broadcasted_iota(jnp.int32, (128, 128), 0) == lax.broadcasted_iota(jnp.int32, (128, 128), 1)

    def spread():
        for p in range(16):
            grep[p] = jnp.broadcast_to(gbuf[p, 0:1, :], (8, 128))
        for pv in range(4):
            for k in range(2):
                a, c = gbuf[8 * k + pv, 1:2, :], gbuf[8 * k + 4 + pv, 1:2, :]
                grep[16 + pv * 2 + k] = jnp.broadcast_to(jnp.where(low_half, a, pltpu.roll(c, 64, 1)), (8, 128))
                grep[24 + pv * 2 + k] = jnp.broadcast_to(jnp.where(low_half, pltpu.roll(a, 64, 1), c), (8, 128))

    def row_tiles(tiles, more=False):
        @pl.loop(0, 128, unroll=4)
        def _(i):
            r = pl.ds(pl.multiple_of(i * 8, 8), 8)
            top = total = None
            tl = list(tiles)
            if more:
                top, total = mrow[r, :], srow[r, :]
            for c in range(0, len(tl), 8):
                stack = jnp.stack([cost[t, r, :] + grep[t] for t in tl[c : c + 8]])
                new = jnp.max(stack, axis=0)
                if top is not None:
                    new = jnp.maximum(top, new)
                part = jnp.sum(jnp.exp2(stack - new[None]), axis=0)
                total = part if top is None else total * jnp.exp2(top - new) + part
                top = new
            mrow[r, :] = top
            srow[r, :] = total

    def row_lse():
        for q in range(8):
            r = slice(128 * q, 128 * q + 128)
            m = mrow[r, :].T
            top = jnp.max(m, axis=0, keepdims=True)
            total = jnp.sum(srow[r, :].T * jnp.exp2(m - top), axis=0, keepdims=True)
            lrow[q // 4, q % 4 : q % 4 + 1, :] = top + jnp.log2(total)

    def row_swap(it):
        swap = remote(lrow, lget.at[it], partner)
        go(swap)
        swap.wait_recv()
        swap.wait_send()
        drop(swap)
        a, c = lrow[...], lget[it]
        top = jnp.maximum(a, c)
        both = top + jnp.log2(jnp.exp2(a - top) + jnp.exp2(c - top))
        frow[...] = LOG2E * wrow[...] - both
        for q in range(8):
            line_ = jnp.broadcast_to(frow[q // 4, q % 4 : q % 4 + 1, :], (128, 128))
            col = jnp.sum(jnp.where(eye, line_, 0.0), axis=1, keepdims=True)
            frep[128 * q : 128 * q + 128, :] = jnp.broadcast_to(col, (128, 128))

    def offset(place):
        return jnp.where(place == 0, 0, jnp.where(place == 1, 3, jnp.where(place == 2, 1, 2)))

    def col_tile(tile):
        top = total = None
        for q in range(8):
            r = slice(128 * q, 128 * q + 128)
            w = (cost[tile, r, :] + frep[r, :]).reshape(16, 8, 128)
            new = jnp.max(w, axis=0)
            if top is not None:
                new = jnp.maximum(top, new)
            part = jnp.sum(jnp.exp2(w - new[None]), axis=0)
            total = part if top is None else total * jnp.exp2(top - new) + part
            top = new
        peak = jnp.max(top, axis=0, keepdims=True)
        mass = jnp.sum(total * jnp.exp2(top - peak), axis=0, keepdims=True)
        return peak + jnp.log2(mass)

    def col_reduce(it):
        base = count[0]
        count[0] += 16

        def give(p):
            to = at(offset(lax.div(p, 4)), offset(rem4(p)), 0, core)
            return remote(lsend.at[p], abuf.at[it, p], to, base + p)

        def places(i):
            pv, k = 3 - lax.div(i, 2), 1 - lax.rem(i, 2)
            return pv, k, 8 * k + pv, 8 * k + 4 + pv

        @pl.loop(0, 8)
        def _(i):
            pv, k, first, second = places(i)
            ltile[0] = col_tile(first)
            ltile[1] = col_tile(second)
            ltile[2] = col_tile(16 + pv * 2 + k)
            ltile[3] = col_tile(24 + pv * 2 + k)
            tb, tc = ltile[2], ltile[3]
            lsend[first, 0:1, :] = ltile[0]
            lsend[first, 1:2, :] = jnp.where(low_half, tb, pltpu.roll(tc, 64, 1))
            lsend[second, 0:1, :] = ltile[1]
            lsend[second, 1:2, :] = jnp.where(low_half, pltpu.roll(tb, 64, 1), tc)

            @pl.when(i > 0)
            def _():
                _, _, a, c = places(i - 1)
                give(c).start()
                give(a).start()

        give(4).start()
        abuf[it, 0] = lsend[0]

        @pl.loop(1, 16)
        def _(p):
            copy = give(p)
            copy.wait_recv()
            copy.wait_send()

        return lse2(abuf[it])

    early = list(range(12)) + list(range(16, 22))
    late = [j for j in range(32) if j not in early]
    spread()
    row_tiles(early)

    for t in trees:
        for ring in t.own + t.near:
            ring.end()
        t.far.end()
    for by in (2, -2):
        pl.semaphore_signal(token, inc=1, device_id=step("z", by), device_id_type=MESH)

    @pl.loop(0, 2)
    def _(i):
        multiply_a(3, i)

    multiply_b(3)

    @pl.loop(0, 4)
    def _(i):
        multiply_c(i)

    row_tiles(late, more=True)
    row_lse()
    row_swap(0)
    zsend[0] = col_reduce(0)
    pl.semaphore_wait(token, 2)
    waits = []
    for dz, peer in line:
        copy = remote(zsend.at[0], bbuf.at[dz], peer)
        go(copy)
        waits.append(copy)
    bbuf[0] = zsend[0]
    for copy in waits:
        copy.wait_recv()
    gsend[...] = own_w - lse2(bbuf[...])
    gbuf[0] = gsend[...]
    waits = []
    place_of, offset_of = (0, 2, 3, 1), (0, 3, 1, 2)
    for p in range(15, 0, -1):
        du, dv = offset_of[p // 4], offset_of[p % 4]
        there = place_of[(4 - du) % 4] * 4 + place_of[(4 - dv) % 4]
        copy = remote(gsend, gbuf.at[there], at(du, dv, 0, core))
        go(copy)
        waits.append((there, count[0] - 1))
    for there, slot in waits:
        remote(gbuf.at[there], gbuf.at[there], partner, slot).wait_recv()

    spread()
    row_tiles(range(32))
    row_lse()
    row_swap(1)
    row_out[...] = frow[core] * (1.0 / TO2)
    zsend[1] = col_reduce(1)
    waits = []
    for dz, peer in line:
        copy = remote(zsend.at[1], fbuf.at[0, dz], peer)
        go(copy)
        waits.append(copy)
    for dz, peer in across:
        copy = remote(zsend.at[1], fbuf.at[1, dz], peer)
        go(copy)
        waits.append(copy)
    fbuf[0, 0] = zsend[1]
    for copy in waits:
        copy.wait_recv()
    hbuf[core] = lse2(fbuf[0])
    hbuf[1 - core] = lse2(fbuf[1])
    total = jnp.zeros((1, 128), jnp.float32)
    within = lax.rem(lanes, 64)
    for c in range(2):
        first, second = hbuf[c, 0:1, :], hbuf[c, 1:2, :]
        out = jnp.zeros((1, 128), jnp.float32)
        for k in range(4):
            w = pltpu.roll(first, (64 * c - 32 * k) % 128, 1)
            w = jnp.where(within < 32, w, pltpu.roll(second, (64 * c + 32 - 16 * k) % 128, 1))
            w = jnp.where(within < 48, w, pltpu.roll(second, (64 * c - 16 - 16 * k) % 128, 1))
            out = jnp.where(zl == k, w, out)
        total = jnp.where(lax.div(lanes, 64) == c, out, total)
    col_out[...] = 0.1 * tlogw_in[...] - (1.0 / TO2) * total

    for copy in started:
        copy.wait_send()


N_SEM = 132 + 12 + 2 + 2 + 32 + 7 + 15 + 15


def shards(source_embed, target_embed, target_init, source_logw, target_logw):
    f32, bf16 = jnp.float32, jnp.bfloat16
    vmem = pl.BlockSpec(memory_space=pltpu.VMEM)
    hbm = pl.BlockSpec(memory_space=pl.ANY)
    row, col = pl.pallas_call(
        kernel,
        out_shape=(jax.ShapeDtypeStruct((4, 128), f32), jax.ShapeDtypeStruct((1, 128), f32)),
        in_specs=[hbm, hbm, vmem, vmem, vmem],
        out_specs=(vmem, vmem),
        scratch_shapes=[
            pltpu.VMEM((1024, D), bf16),
            pltpu.VMEM((R, R, R, 32, D), bf16),
            pltpu.VMEM((R, R, R, 16, D), bf16),
            pltpu.VMEM((R, R, R, 16, D), bf16),
            pltpu.VMEM((R, R, R, 2, 128), f32),
            pltpu.VMEM((32, 1024, 128), f32),
            pltpu.VMEM((32, 8, 128), f32),
            pltpu.VMEM((2, 128), f32),
            pltpu.VMEM((16, 2, 128), f32),
            pltpu.VMEM((1024, 128), f32),
            pltpu.VMEM((1024, 128), f32),
            pltpu.VMEM((1024, 128), f32),
            pltpu.VMEM((2, 4, 128), f32),
            pltpu.VMEM((2, 4, 128), f32),
            pltpu.VMEM((2, 2, 4, 128), f32),
            pltpu.VMEM((2, 4, 128), f32),
            pltpu.VMEM((4, 1, 128), f32),
            pltpu.VMEM((16, 2, 128), f32),
            pltpu.VMEM((2, 16, 2, 128), f32),
            pltpu.VMEM((2, 2, 128), f32),
            pltpu.VMEM((8, 2, 128), f32),
            pltpu.VMEM((2, 8, 2, 128), f32),
            pltpu.VMEM((2, 2, 128), f32),
            pltpu.SemaphoreType.DMA((N_SEM,)),
            pltpu.SemaphoreType.DMA((N_SEM,)),
            pltpu.SemaphoreType.DMA((4,)),
            pltpu.SemaphoreType.REGULAR,
        ],
        compiler_params=pltpu.CompilerParams(
            collective_id=0, has_side_effects=True, vmem_limit_bytes=60 * 2**20
        ),
    )(
        source_embed, target_embed, target_init.reshape(1, 128),
        source_logw.reshape(4, 128), target_logw.reshape(1, 128),
    )
    return row.reshape(512), col.reshape(128)


def solution(mesh):
    in_specs = (P(("blk", "grp"), None), P("blk", None), P("blk"), P(("blk", "grp")), P("blk"))
    out_specs = (P(("blk", "grp")), P("blk"))
    return jax.shard_map(shards, mesh=mesh, in_specs=in_specs, out_specs=out_specs, check_vma=False)
```

```python
import math

import jax
import jax.numpy as jnp
from jax import lax
from jax.experimental import pallas as pl
from jax.experimental.pallas import tpu as pltpu
from jax.sharding import PartitionSpec as P

D = 768
LOG2E = math.log2(math.e)
TO2 = 10.0 * LOG2E
SCALE = TO2 / math.sqrt(D)
NZ = 8
R = 4
MESH = pl.DeviceIdType.MESH


def lse2(stack):
    top = jnp.max(stack, axis=0)
    return top + jnp.log2(jnp.sum(jnp.exp2(stack - top[None]), axis=0))


def rem4(v):
    return lax.rem(v, 4)


def kernel(
    src_in, tgt_in, init_in, slogw_in, tlogw_in, row_out, col_out,
    src, buf_a, buf_b, aux, cost, grep, gsend, gbuf, mrow, srow, frep, wrow, lrow, lget, frow,
    ltile, lsend, abuf, zsend, bbuf, fbuf, hbuf,
    send, recv, loc, token,
):
    b, g = lax.axis_index("blk"), lax.axis_index("grp")
    core, zh = lax.rem(g, 2), lax.div(g, 2)
    zl, x, y = lax.div(b, 16), rem4(lax.div(b, 4)), rem4(b)
    z = zh * 4 + zl
    x_in, x_out = x + 1 - 2 * lax.rem(x, 2), 3 - x

    def dev(px, py, pz, pc):
        return (rem4(pz) * 16 + px * 4 + py, lax.div(pz, 4) * 2 + pc)

    def at(out, dy, dz, pc):
        px = jnp.where(out == 1, x_out, x)
        return dev(px, rem4(y + dy + 4), lax.rem(z + dz + NZ, NZ), pc)

    def step(dim, by):
        return at(0, by if dim == "y" else 0, by if dim == "z" else 0, core)

    partner = at(0, 0, 0, 1 - core)
    mates = [partner, dev(x_in, y, z, core), dev(x_in, y, z, 1 - core)]
    opposite = at(1, 0, 0, core)
    line = [(dz, at(0, 0, dz, core)) for dz in range(1, NZ)]
    across = [(dz, at(0, 0, dz, 1 - core)) for dz in range(NZ)]

    barrier = pltpu.get_barrier_semaphore()
    peers = [step(d, by) for d in ("y", "z") for by in (1, -1)] + mates + [opposite]
    for peer in peers:
        pl.semaphore_signal(barrier, inc=1, device_id=peer, device_id_type=MESH)

    half = pl.multiple_of(core * 64, 64)
    locals_ = [
        pltpu.make_async_copy(tgt_in.at[pl.ds(half, 32), :], buf_a.at[0, 0, 0], loc.at[0]),
        pltpu.make_async_copy(tgt_in.at[pl.ds(half + 32, 32), :], buf_b.at[0, 0, 0], loc.at[1]),
        pltpu.make_async_copy(src_in, src.at[pl.ds(0, 512), :], loc.at[2]),
    ]
    for copy in locals_:
        copy.start()
    aux[0, 0, 0] = jnp.concatenate([init_in[...], tlogw_in[...]], axis=0)
    wrow[0] = slogw_in[...]

    count = [0]
    started = []

    def remote(src_ref, dst_ref, to, slot=None):
        if slot is None:
            slot = count[0]
            count[0] += 1
        return pltpu.make_async_remote_copy(
            src_ref=src_ref, dst_ref=dst_ref, send_sem=send.at[slot], recv_sem=recv.at[slot],
            device_id=to, device_id_type=MESH,
        )

    def go(copy):
        copy.start()
        started.append(copy)

    def drop(copy):
        started[:] = [c for c in started if c is not copy]

    class Ring:
        def __init__(self, dim, unit, low=None, high=None):
            self.dim, self.unit = dim, unit
            self.low, self.high = low or unit, high
            self.base = count[0]
            count[0] += 4
            self.up, self.down = step(dim, 1), step(dim, -1)

        def begin(self):
            go(remote(self.unit(0), self.unit(1), self.up, self.base))
            go(remote(self.unit(0), self.unit(2), self.down, self.base + 1))

        def mid(self):
            remote(self.unit(1), self.unit(1), self.up, self.base).wait_recv()
            go(remote(self.low(1), self.low(3), self.up, self.base + 2))
            remote(self.unit(2), self.unit(2), self.down, self.base + 1).wait_recv()
            if self.high is not None:
                go(remote(self.high(2), self.high(3), self.down, self.base + 3))

        def end(self):
            remote(self.low(3), self.low(3), self.up, self.base + 2).wait_recv()
            if self.high is not None:
                remote(self.high(3), self.high(3), self.down, self.base + 3).wait_recv()

    class Tree:
        def __init__(self, buf, d1, d2):
            top, end = pl.ds(0, 16), pl.ds(16, 16)
            self.first = remote(buf.at[0, 0, 0], buf.at[0, 0, 1], opposite)

            def single(dim, place):
                return Ring(
                    dim, lambda p: buf.at[place(p)], lambda p: buf.at[place(p) + (top,)], lambda p: buf.at[place(p) + (end,)]
                )

            self.two = [single(d1, lambda p, k=k: (0, p, k)) for k in range(2)]
            self.own = [single(d2, lambda p, k=k: (p, 0, k)) for k in range(2)]
            self.near = [
                Ring(d2, lambda p, k=k: buf.at[p, pl.ds(1, 2), k], lambda p, k=k: buf.at[p, 1, k], lambda p, k=k: buf.at[p, 2, k])
                for k in range(2)
            ]
            self.far = [single(d2, lambda p, k=k: (p, 3, k)) for k in range(2)]

    trees = [Tree(buf_a, "z", "y"), Tree(buf_b, "y", "z")]
    aux_first = remote(aux.at[0, 0, 0], aux.at[0, 0, 1], opposite)
    aux_rings = [Ring("y", lambda p: aux.at[0, p]), Ring("z", lambda p: aux.at[p])]

    def rows(slot, k):
        return src.at[pl.ds(512 * slot + 128 * k, 128), :]

    to_mate = [remote(rows(0, k), rows(2, k), mates[1]) for k in range(4)]
    to_partner = remote(src.at[pl.ds(0, 512), :], src.at[pl.ds(512, 512), :], partner)
    relay = [remote(rows(2, k), rows(3, k), partner) for k in range(4)]
    to_all = [remote(wrow.at[0], wrow.at[k + 1], mates[k]) for k in range(3)]

    for copy in locals_[:2]:
        copy.wait()
    pl.semaphore_wait(barrier, len(peers))

    for t in trees:
        go(t.first)
        t.two[0].begin()
        t.own[0].begin()
    go(aux_first)
    locals_[2].wait()
    for copy in to_mate:
        go(copy)
    go(to_partner)
    for copy in to_all:
        go(copy)

    for t in trees:
        t.first.wait_recv()
        t.two[1].begin()
        t.own[1].begin()
    aux_first.wait_recv()
    aux_rings[0].begin()
    for t in trees:
        t.two[0].mid()
        t.near[0].begin()
    aux_rings[0].mid()
    for t in trees:
        t.two[1].mid()
        t.near[1].begin()
    aux_rings[0].end()
    aux_rings[1].begin()
    for t in trees:
        t.two[0].end()
        t.far[0].begin()
    to_mate[0].wait_recv()
    go(relay[0])
    for t in trees:
        t.two[1].end()
        t.far[1].begin()
    for k in range(2):
        for t in trees:
            t.own[k].mid()
    aux_rings[1].mid()
    for copy in to_all:
        copy.wait_recv()
    to_partner.wait_recv()

    zplace = []
    for k in range(4):
        r = rem4(k - zl + 4)
        zplace.append(jnp.where(r == 0, 0, jnp.where(r == 3, 1, jnp.where(r == 1, 2, 3))))

    def multiply(h, pieces, tiles):
        r = slice(1024 * h, 1024 * h + 1024)
        out = SCALE * lax.dot_general(
            src[r, :], jnp.concatenate(pieces, axis=0), (((1,), (1,)), ((), ())), preferred_element_type=jnp.float32
        )
        cost[tiles[0], r, :] = out[:, :128]
        cost[tiles[1], r, :] = out[:, 128:]

    def multiply_a(h, pv):
        multiply(h, [buf_a[pv, zp, k] for k in range(2) for zp in zplace], (pv, 4 + pv))

    def multiply_b(h, pz):
        multiply(h, [buf_b[pz, pv, k] for k in range(2) for pv in range(4)], (8 + 2 * pz, 9 + 2 * pz))

    for t in trees:
        t.near[0].mid()
    multiply_a(0, 0)
    for t in trees:
        t.near[1].mid()
    to_mate[1].wait_recv()
    go(relay[1])
    multiply_b(0, 0)
    for k in range(2):
        for t in trees:
            t.far[k].mid()
    aux_rings[1].end()
    to_mate[2].wait_recv()
    go(relay[2])

    @pl.loop(1, 3)
    def _(i):
        multiply_a(0, i)
        multiply_b(0, i)

    to_mate[3].wait_recv()
    go(relay[3])

    lanes = lax.broadcasted_iota(jnp.int32, (1, 128), 1)
    low_half = lanes < 64
    chunk = lax.div(lanes, 32)

    def group_of(blocks):
        first = second = jnp.zeros((1, 128), jnp.float32)
        for k, block in enumerate(blocks):
            w = jnp.where(core == 0, block, pltpu.roll(block, 64, 1))
            first = jnp.where(chunk == k, pltpu.roll(w, (k * 32) % 128, 1), first)
            second = jnp.where(chunk == k, pltpu.roll(w, (k * 32 - 32) % 128, 1), second)
        return jnp.concatenate([first, second], axis=0)

    for k in range(2):
        for pv in range(4):
            gbuf[k * 4 + pv] = TO2 * group_of([aux[zp, pv, k, 0:1, :] for zp in zplace])
    own_w = LOG2E * group_of([aux[zp, 0, 0, 1:2, :] for zp in zplace])

    eye = lax.broadcasted_iota(jnp.int32, (128, 128), 0) == lax.broadcasted_iota(jnp.int32, (128, 128), 1)

    def spread():
        for p in range(8):
            grep[p] = jnp.broadcast_to(gbuf[p, 0:1, :], (8, 128))
        for n, zp in enumerate(zplace):
            for k in range(2):
                tile = jnp.zeros((1, 128), jnp.float32)
                for pv in range(4):
                    w = pltpu.roll(gbuf[k * 4 + pv, 1:2, :], (32 * pv - 32 * n) % 128, 1)
                    tile = jnp.where(chunk == pv, w, tile)
                grep[8 + zp * 2 + k] = jnp.broadcast_to(tile, (8, 128))

    def row_tiles(tiles, more=False):
        @pl.loop(0, 256, unroll=8)
        def _(i):
            r = pl.ds(pl.multiple_of(i * 8, 8), 8)
            top = total = None
            tl = list(tiles)
            if more:
                top, total = mrow[r, :], srow[r, :]
            for c in range(0, len(tl), 8):
                stack = jnp.stack([cost[t, r, :] + grep[t] for t in tl[c : c + 8]])
                new = jnp.max(stack, axis=0)
                if top is not None:
                    new = jnp.maximum(top, new)
                part = jnp.sum(jnp.exp2(stack - new[None]), axis=0)
                total = part if top is None else total * jnp.exp2(top - new) + part
                top = new
            mrow[r, :] = top
            srow[r, :] = total

    def row_lse():
        for q in range(16):
            r = slice(128 * q, 128 * q + 128)
            m = mrow[r, :].T
            top = jnp.max(m, axis=0, keepdims=True)
            total = jnp.sum(srow[r, :].T * jnp.exp2(m - top), axis=0, keepdims=True)
            lrow[q // 4, q % 4 : q % 4 + 1, :] = top + jnp.log2(total)

    def row_swap(it):
        swaps = [remote(lrow, lget.at[it, k], mates[k]) for k in range(3)]
        for copy in swaps:
            copy.start()
        for copy in swaps:
            copy.wait_recv()
            copy.wait_send()
        for slot in range(4):
            terms = [lrow[slot]] + [lget[it, k, slot ^ (k + 1)] for k in range(3)]
            frow[slot] = LOG2E * wrow[slot] - lse2(jnp.stack(terms))
        for q in range(16):
            line_ = jnp.broadcast_to(frow[q // 4, q % 4 : q % 4 + 1, :], (128, 128))
            col = jnp.sum(jnp.where(eye, line_, 0.0), axis=1, keepdims=True)
            frep[128 * q : 128 * q + 128, :] = jnp.broadcast_to(col, (128, 128))

    def offset(place):
        return jnp.where(place == 0, 0, jnp.where(place == 1, 3, jnp.where(place == 2, 1, 2)))

    def col_tile(tile):
        top = total = None
        for q in range(16):
            r = slice(128 * q, 128 * q + 128)
            w = (cost[tile, r, :] + frep[r, :]).reshape(16, 8, 128)
            new = jnp.max(w, axis=0)
            if top is not None:
                new = jnp.maximum(top, new)
            part = jnp.sum(jnp.exp2(w - new[None]), axis=0)
            total = part if top is None else total * jnp.exp2(top - new) + part
            top = new
        peak = jnp.max(top, axis=0, keepdims=True)
        mass = jnp.sum(total * jnp.exp2(top - peak), axis=0, keepdims=True)
        return peak + jnp.log2(mass)

    def col_reduce(it):
        base = count[0]
        count[0] += 8

        def give(p):
            to = at(lax.div(p, 4), offset(rem4(p)), 0, core)
            return remote(lsend.at[p], abuf.at[it, p], to, base + p)

        def group(i):
            return (1 - lax.rem(i, 2)) * 4 + 3 - lax.div(i, 2)

        @pl.loop(0, 8)
        def _(i):
            ltile[i] = col_tile(8 + i)

        for k in range(2):
            for pv in range(4):
                line_ = jnp.zeros((1, 128), jnp.float32)
                for n, zp in enumerate(zplace):
                    w = pltpu.roll(ltile[zp * 2 + k], (32 * n - 32 * pv) % 128, 1)
                    line_ = jnp.where(chunk == n, w, line_)
                lsend[k * 4 + pv, 1:2, :] = line_

        @pl.loop(0, 8)
        def _(i):
            p = group(i)
            lsend[p, 0:1, :] = col_tile(p)

            @pl.when(i > 0)
            def _():
                give(group(i - 1)).start()

        abuf[it, 0] = lsend[0]

        @pl.loop(1, 8)
        def _(p):
            copy = give(p)
            copy.wait_recv()
            copy.wait_send()

        return lse2(abuf[it])

    for copy in relay:
        copy.wait_recv()

    @pl.loop(0, 3)
    def _(i):
        multiply_a(1, i)
        multiply_b(1, i)

    for t in trees:
        for ring in t.own + t.near + t.far:
            ring.end()
    for by in (2, -2):
        pl.semaphore_signal(token, inc=1, device_id=step("z", by), device_id_type=MESH)
    for n in range(2):
        multiply_a(n, 3)
        multiply_b(n, 3)

    spread()
    row_tiles(range(16))
    row_lse()
    row_swap(0)
    zsend[0] = col_reduce(0)
    pl.semaphore_wait(token, 2)
    waits = []
    for dz, peer in line:
        copy = remote(zsend.at[0], bbuf.at[dz], peer)
        go(copy)
        waits.append(copy)
    bbuf[0] = zsend[0]
    for copy in waits:
        copy.wait_recv()
    gsend[...] = own_w - lse2(bbuf[...])
    gbuf[0] = gsend[...]
    waits = []
    place_of, offset_of = (0, 2, 3, 1), (0, 3, 1, 2)
    for p in range(7, 0, -1):
        out, dy = p // 4, offset_of[p % 4]
        there = out * 4 + place_of[(4 - dy) % 4]
        copy = remote(gsend, gbuf.at[there], at(out, dy, 0, core))
        go(copy)
        waits.append((there, count[0] - 1))
    for there, slot in waits:
        remote(gbuf.at[there], gbuf.at[there], partner, slot).wait_recv()

    spread()
    row_tiles(range(16))
    row_lse()
    row_swap(1)
    row_out[...] = frow[0] * (1.0 / TO2)
    zsend[1] = col_reduce(1)
    waits = []
    for dz, peer in line:
        copy = remote(zsend.at[1], fbuf.at[0, dz], peer)
        go(copy)
        waits.append(copy)
    for dz, peer in across:
        copy = remote(zsend.at[1], fbuf.at[1, dz], peer)
        go(copy)
        waits.append(copy)
    fbuf[0, 0] = zsend[1]
    for copy in waits:
        copy.wait_recv()
    hbuf[core] = lse2(fbuf[0])
    hbuf[1 - core] = lse2(fbuf[1])
    total = jnp.zeros((1, 128), jnp.float32)
    within = lax.rem(lanes, 64)
    for c in range(2):
        first, second = hbuf[c, 0:1, :], hbuf[c, 1:2, :]
        out = jnp.zeros((1, 128), jnp.float32)
        for k in range(4):
            w = jnp.where(
                within < 32,
                pltpu.roll(first, (64 * c - 32 * k) % 128, 1),
                pltpu.roll(second, (64 * c + 32 - 32 * k) % 128, 1),
            )
            out = jnp.where(zl == k, w, out)
        total = jnp.where(lax.div(lanes, 64) == c, out, total)
    col_out[...] = 0.1 * tlogw_in[...] - (1.0 / TO2) * total

    for copy in started:
        copy.wait_send()


N_SEM = 66 + 9 + 12 + 6 + 16 + 7 + 7 + 15


def shards(source_embed, target_embed, target_init, source_logw, target_logw):
    f32, bf16 = jnp.float32, jnp.bfloat16
    vmem = pl.BlockSpec(memory_space=pltpu.VMEM)
    hbm = pl.BlockSpec(memory_space=pl.ANY)
    row, col = pl.pallas_call(
        kernel,
        out_shape=(jax.ShapeDtypeStruct((4, 128), f32), jax.ShapeDtypeStruct((1, 128), f32)),
        in_specs=[hbm, hbm, vmem, vmem, vmem],
        out_specs=(vmem, vmem),
        scratch_shapes=[
            pltpu.VMEM((2048, D), bf16),
            pltpu.VMEM((R, R, 2, 32, D), bf16),
            pltpu.VMEM((R, R, 2, 32, D), bf16),
            pltpu.VMEM((R, R, 2, 2, 128), f32),
            pltpu.VMEM((16, 2048, 128), f32),
            pltpu.VMEM((16, 8, 128), f32),
            pltpu.VMEM((2, 128), f32),
            pltpu.VMEM((8, 2, 128), f32),
            pltpu.VMEM((2048, 128), f32),
            pltpu.VMEM((2048, 128), f32),
            pltpu.VMEM((2048, 128), f32),
            pltpu.VMEM((4, 4, 128), f32),
            pltpu.VMEM((4, 4, 128), f32),
            pltpu.VMEM((2, 3, 4, 4, 128), f32),
            pltpu.VMEM((4, 4, 128), f32),
            pltpu.VMEM((8, 1, 128), f32),
            pltpu.VMEM((8, 2, 128), f32),
            pltpu.VMEM((2, 8, 2, 128), f32),
            pltpu.VMEM((2, 2, 128), f32),
            pltpu.VMEM((8, 2, 128), f32),
            pltpu.VMEM((2, 8, 2, 128), f32),
            pltpu.VMEM((2, 2, 128), f32),
            pltpu.SemaphoreType.DMA((N_SEM,)),
            pltpu.SemaphoreType.DMA((N_SEM,)),
            pltpu.SemaphoreType.DMA((4,)),
            pltpu.SemaphoreType.REGULAR,
        ],
        compiler_params=pltpu.CompilerParams(
            collective_id=0, has_side_effects=True, vmem_limit_bytes=60 * 2**20
        ),
    )(
        source_embed, target_embed, target_init.reshape(1, 128),
        source_logw.reshape(4, 128), target_logw.reshape(1, 128),
    )
    return row.reshape(512), col.reshape(128)


def solution(mesh):
    in_specs = (P(("blk", "grp"), None), P("blk", None), P("blk"), P(("blk", "grp")), P("blk"))
    out_specs = (P(("blk", "grp")), P("blk"))
    return jax.shard_map(shards, mesh=mesh, in_specs=in_specs, out_specs=out_specs, check_vma=False)
```

```python
import math

import jax
import jax.numpy as jnp
from jax import lax
from jax.experimental import pallas as pl
from jax.experimental.pallas import tpu as pltpu
from jax.sharding import PartitionSpec as P

D = 768
LOG2E = math.log2(math.e)
TO2 = 10.0 * LOG2E
SCALE = TO2 / math.sqrt(D)
NZ = 8
R = 4
MESH = pl.DeviceIdType.MESH


def lse2(stack):
    top = jnp.max(stack, axis=0)
    return top + jnp.log2(jnp.sum(jnp.exp2(stack - top[None]), axis=0))


def rem4(v):
    return lax.rem(v, 4)


def kernel(
    src_in, tgt_in, init_in, slogw_in, tlogw_in, row_out, col_out,
    src, buf_a, buf_b, aux, cost, grep, gsend, gbuf, mrow, srow, frep, wrow, lrow, lget, frow,
    ctop, csum, ltile, lsend, abuf, zsend, bbuf, fbuf, hbuf,
    send, recv, loc, token,
):
    b, g = lax.axis_index("blk"), lax.axis_index("grp")
    core, zh = lax.rem(g, 2), lax.div(g, 2)
    zl, x, y = lax.div(b, 16), rem4(lax.div(b, 4)), rem4(b)
    z = zh * 4 + zl
    x_in, x_out = x + 1 - 2 * lax.rem(x, 2), 3 - x

    def dev(px, py, pz, pc):
        return (rem4(pz) * 16 + px * 4 + py, lax.div(pz, 4) * 2 + pc)

    def at(out, dy, dz, pc):
        px = jnp.where(out == 1, x_out, x)
        return dev(px, rem4(y + dy + 4), lax.rem(z + dz + NZ, NZ), pc)

    def step(dim, by):
        return at(0, by if dim == "y" else 0, by if dim == "z" else 0, core)

    partner = at(0, 0, 0, 1 - core)
    mates = [partner, dev(x_in, y, z, core), dev(x_in, y, z, 1 - core)]
    opposite = at(1, 0, 0, core)
    line = [(dz, at(0, 0, dz, core)) for dz in range(1, NZ)]
    across = [(dz, at(0, 0, dz, 1 - core)) for dz in range(NZ)]

    barrier = pltpu.get_barrier_semaphore()
    peers = [step(d, by) for d in ("y", "z") for by in (1, -1)] + mates + [opposite]
    for peer in peers:
        pl.semaphore_signal(barrier, inc=1, device_id=peer, device_id_type=MESH)

    half = pl.multiple_of(core * 64, 64)
    locals_ = [
        pltpu.make_async_copy(tgt_in.at[pl.ds(half, 32), :], buf_a.at[0, 0, 0], loc.at[0]),
        pltpu.make_async_copy(tgt_in.at[pl.ds(half + 32, 32), :], buf_b.at[0, 0, 0], loc.at[1]),
        pltpu.make_async_copy(src_in, src.at[pl.ds(0, 512), :], loc.at[2]),
    ]
    for copy in locals_:
        copy.start()
    aux[0, 0, 0] = jnp.concatenate([init_in[...], tlogw_in[...]], axis=0)
    wrow[0] = slogw_in[...]

    count = [0]
    started = []

    def remote(src_ref, dst_ref, to, slot=None):
        if slot is None:
            slot = count[0]
            count[0] += 1
        return pltpu.make_async_remote_copy(
            src_ref=src_ref, dst_ref=dst_ref, send_sem=send.at[slot], recv_sem=recv.at[slot],
            device_id=to, device_id_type=MESH,
        )

    def go(copy):
        copy.start()
        started.append(copy)

    def drop(copy):
        started[:] = [c for c in started if c is not copy]

    class Ring:
        def __init__(self, dim, unit, low=None, high=None):
            self.dim, self.unit = dim, unit
            self.low, self.high = low or unit, high
            self.base = count[0]
            count[0] += 4
            self.up, self.down = step(dim, 1), step(dim, -1)

        def begin(self):
            go(remote(self.unit(0), self.unit(1), self.up, self.base))
            go(remote(self.unit(0), self.unit(2), self.down, self.base + 1))

        def mid(self):
            remote(self.unit(1), self.unit(1), self.up, self.base).wait_recv()
            go(remote(self.low(1), self.low(3), self.up, self.base + 2))
            remote(self.unit(2), self.unit(2), self.down, self.base + 1).wait_recv()
            if self.high is not None:
                go(remote(self.high(2), self.high(3), self.down, self.base + 3))

        def end(self):
            remote(self.low(3), self.low(3), self.up, self.base + 2).wait_recv()
            if self.high is not None:
                remote(self.high(3), self.high(3), self.down, self.base + 3).wait_recv()

    class Tree:
        def __init__(self, buf, d1, d2):
            top, end = pl.ds(0, 16), pl.ds(16, 16)
            self.first = remote(buf.at[0, 0, 0], buf.at[0, 0, 1], opposite)

            def single(dim, place):
                return Ring(
                    dim, lambda p: buf.at[place(p)], lambda p: buf.at[place(p) + (top,)], lambda p: buf.at[place(p) + (end,)]
                )

            self.two = [single(d1, lambda p, k=k: (0, p, k)) for k in range(2)]
            self.own = [single(d2, lambda p, k=k: (p, 0, k)) for k in range(2)]
            self.near = [
                Ring(d2, lambda p, k=k: buf.at[p, pl.ds(1, 2), k], lambda p, k=k: buf.at[p, 1, k], lambda p, k=k: buf.at[p, 2, k])
                for k in range(2)
            ]
            self.far = [single(d2, lambda p, k=k: (p, 3, k)) for k in range(2)]

    trees = [Tree(buf_a, "z", "y"), Tree(buf_b, "y", "z")]
    aux_first = remote(aux.at[0, 0, 0], aux.at[0, 0, 1], opposite)
    aux_rings = [Ring("y", lambda p: aux.at[0, p]), Ring("z", lambda p: aux.at[p])]

    def rows(slot, k):
        return src.at[pl.ds(512 * slot + 128 * k, 128), :]

    to_mate = [remote(rows(0, k), rows(2, k), mates[1]) for k in range(4)]
    to_partner = remote(src.at[pl.ds(0, 512), :], src.at[pl.ds(512, 512), :], partner)
    relay = [remote(rows(2, k), rows(3, k), partner) for k in range(4)]
    to_all = [remote(wrow.at[0], wrow.at[k + 1], mates[k]) for k in range(3)]

    for copy in locals_[:2]:
        copy.wait()
    pl.semaphore_wait(barrier, len(peers))

    for t in trees:
        go(t.first)
        t.two[0].begin()
        t.own[0].begin()
    go(aux_first)
    locals_[2].wait()
    for copy in to_mate:
        go(copy)
    go(to_partner)
    for copy in to_all:
        go(copy)

    for t in trees:
        t.first.wait_recv()
        t.two[1].begin()
        t.own[1].begin()
    aux_first.wait_recv()
    aux_rings[0].begin()
    for t in trees:
        t.two[0].mid()
        t.near[0].begin()
    aux_rings[0].mid()
    for t in trees:
        t.two[1].mid()
        t.near[1].begin()
    aux_rings[0].end()
    aux_rings[1].begin()
    for t in trees:
        t.two[0].end()
        t.far[0].begin()
    to_mate[0].wait_recv()
    go(relay[0])
    for t in trees:
        t.two[1].end()
        t.far[1].begin()
    for k in range(2):
        for t in trees:
            t.own[k].mid()
    aux_rings[1].mid()
    for copy in to_all:
        copy.wait_recv()
    to_partner.wait_recv()

    zplace = []
    for k in range(4):
        r = rem4(k - zl + 4)
        zplace.append(jnp.where(r == 0, 0, jnp.where(r == 3, 1, jnp.where(r == 1, 2, 3))))

    def multiply(h, pieces, tiles):
        r = slice(1024 * h, 1024 * h + 1024)
        out = SCALE * lax.dot_general(
            src[r, :], jnp.concatenate(pieces, axis=0), (((1,), (1,)), ((), ())), preferred_element_type=jnp.float32
        )
        cost[tiles[0], r, :] = out[:, :128]
        cost[tiles[1], r, :] = out[:, 128:]

    def multiply_a(h, pv):
        multiply(h, [buf_a[pv, zp, k] for k in range(2) for zp in zplace], (pv, 4 + pv))

    def multiply_b(h, pz):
        multiply(h, [buf_b[pz, pv, k] for k in range(2) for pv in range(4)], (8 + 2 * pz, 9 + 2 * pz))

    for t in trees:
        t.near[0].mid()
    multiply_a(0, 0)
    for t in trees:
        t.near[1].mid()
    to_mate[1].wait_recv()
    go(relay[1])
    multiply_b(0, 0)
    for k in range(2):
        for t in trees:
            t.far[k].mid()
    aux_rings[1].end()
    to_mate[2].wait_recv()
    go(relay[2])

    @pl.loop(1, 3)
    def _(i):
        multiply_a(0, i)
        multiply_b(0, i)

    to_mate[3].wait_recv()
    go(relay[3])

    lanes = lax.broadcasted_iota(jnp.int32, (1, 128), 1)
    low_half = lanes < 64
    chunk = lax.div(lanes, 32)

    def group_of(blocks):
        first = second = jnp.zeros((1, 128), jnp.float32)
        for k, block in enumerate(blocks):
            w = jnp.where(core == 0, block, pltpu.roll(block, 64, 1))
            first = jnp.where(chunk == k, pltpu.roll(w, (k * 32) % 128, 1), first)
            second = jnp.where(chunk == k, pltpu.roll(w, (k * 32 - 32) % 128, 1), second)
        return jnp.concatenate([first, second], axis=0)

    for k in range(2):
        for pv in range(4):
            gbuf[k * 4 + pv] = TO2 * group_of([aux[zp, pv, k, 0:1, :] for zp in zplace])
    own_w = LOG2E * group_of([aux[zp, 0, 0, 1:2, :] for zp in zplace])

    eye = lax.broadcasted_iota(jnp.int32, (128, 128), 0) == lax.broadcasted_iota(jnp.int32, (128, 128), 1)

    def spread():
        for p in range(8):
            grep[p] = jnp.broadcast_to(gbuf[p, 0:1, :], (8, 128))
        for n, zp in enumerate(zplace):
            for k in range(2):
                tile = jnp.zeros((1, 128), jnp.float32)
                for pv in range(4):
                    w = pltpu.roll(gbuf[k * 4 + pv, 1:2, :], (32 * pv - 32 * n) % 128, 1)
                    tile = jnp.where(chunk == pv, w, tile)
                grep[8 + zp * 2 + k] = jnp.broadcast_to(tile, (8, 128))

    halves = [lax.rem(x + k, 2) for k in range(2)]

    def row_pass(hd):
        @pl.loop(0, 128, unroll=8)
        def _(i):
            r = pl.ds(pl.multiple_of(1024 * hd + i * 8, 8), 8)
            top = total = None
            for c in range(0, 16, 8):
                stack = jnp.stack([cost[t, r, :] + grep[t] for t in range(c, c + 8)])
                new = jnp.max(stack, axis=0)
                if top is not None:
                    new = jnp.maximum(top, new)
                part = jnp.sum(jnp.exp2(stack - new[None]), axis=0)
                total = part if top is None else total * jnp.exp2(top - new) + part
                top = new
            mrow[r, :] = top
            srow[r, :] = total

        for k in range(2):
            for q in range(4):
                r = pl.ds(pl.multiple_of(1024 * hd + 512 * k + 128 * q, 128), 128)
                m = mrow[r, :].T
                top = jnp.max(m, axis=0, keepdims=True)
                total = jnp.sum(srow[r, :].T * jnp.exp2(m - top), axis=0, keepdims=True)
                lrow[2 * hd + k, q : q + 1, :] = top + jnp.log2(total)

    def swap_rows(it, hd):
        swaps = []
        for k in range(3):
            theirs = hd if k == 0 else 1 - hd
            mine = pl.ds(2 * hd, 2)
            copy = remote(lrow.at[mine], lget.at[it, k, mine], mates[k])
            copy.start()
            other = lget.at[it, k, pl.ds(2 * theirs, 2)]
            swaps.append((copy, remote(other, other, mates[k], count[0] - 1)))
        return swaps

    def finish_rows(it, hd, swaps):
        for copy, arrival in swaps:
            arrival.wait_recv()
            copy.wait_send()
        for k in range(2):
            slot = 2 * hd + k
            terms = [
                lrow[slot], lget[it, 0, 2 * hd + 1 - k], lget[it, 1, 2 * (1 - hd) + k], lget[it, 2, 2 * (1 - hd) + 1 - k],
            ]
            frow[slot] = LOG2E * wrow[slot] - lse2(jnp.stack(terms))
            for q in range(4):
                r = pl.ds(pl.multiple_of(1024 * hd + 512 * k + 128 * q, 128), 128)
                line_ = jnp.broadcast_to(frow[slot, q : q + 1, :], (128, 128))
                col = jnp.sum(jnp.where(eye, line_, 0.0), axis=1, keepdims=True)
                frep[r, :] = jnp.broadcast_to(col, (128, 128))

    def sweep(it):
        row_pass(halves[0])
        early = swap_rows(it, halves[0])
        row_pass(halves[1])
        late = swap_rows(it, halves[1])
        finish_rows(it, halves[0], early)

        @pl.loop(0, 16, unroll=2)
        def _(t):
            ctop[t], csum[t] = col_half(t, halves[0], None, None)

        finish_rows(it, halves[1], late)
        return col_reduce(it)

    def offset(place):
        return jnp.where(place == 0, 0, jnp.where(place == 1, 3, jnp.where(place == 2, 1, 2)))

    def col_half(tile, hd, top, total):
        for q in range(8):
            r = pl.ds(pl.multiple_of(1024 * hd + 128 * q, 128), 128)
            w = (cost[tile, r, :] + frep[r, :]).reshape(16, 8, 128)
            new = jnp.max(w, axis=0)
            if top is not None:
                new = jnp.maximum(top, new)
            part = jnp.sum(jnp.exp2(w - new[None]), axis=0)
            total = part if top is None else total * jnp.exp2(top - new) + part
            top = new
        return top, total

    def col_tile(tile):
        top, total = col_half(tile, halves[1], ctop[tile], csum[tile])
        peak = jnp.max(top, axis=0, keepdims=True)
        mass = jnp.sum(total * jnp.exp2(top - peak), axis=0, keepdims=True)
        return peak + jnp.log2(mass)

    def col_reduce(it):
        base = count[0]
        count[0] += 8

        def give(p):
            to = at(lax.div(p, 4), offset(rem4(p)), 0, core)
            return remote(lsend.at[p], abuf.at[it, p], to, base + p)

        def group(i):
            return (1 - lax.rem(i, 2)) * 4 + 3 - lax.div(i, 2)

        @pl.loop(0, 8, unroll=2)
        def _(i):
            ltile[i] = col_tile(8 + i)

        for k in range(2):
            for pv in range(4):
                line_ = jnp.zeros((1, 128), jnp.float32)
                for n, zp in enumerate(zplace):
                    w = pltpu.roll(ltile[zp * 2 + k], (32 * n - 32 * pv) % 128, 1)
                    line_ = jnp.where(chunk == n, w, line_)
                lsend[k * 4 + pv, 1:2, :] = line_

        @pl.loop(0, 8)
        def _(i):
            p = group(i)
            lsend[p, 0:1, :] = col_tile(p)

            @pl.when(i > 0)
            def _():
                give(group(i - 1)).start()

        abuf[it, 0] = lsend[0]

        @pl.loop(1, 8)
        def _(p):
            copy = give(p)
            copy.wait_recv()
            copy.wait_send()

        return lse2(abuf[it])

    for copy in relay:
        copy.wait_recv()

    @pl.loop(0, 3)
    def _(i):
        multiply_a(1, i)
        multiply_b(1, i)

    for t in trees:
        for ring in t.own + t.near + t.far:
            ring.end()
    for by in (2, -2):
        pl.semaphore_signal(token, inc=1, device_id=step("z", by), device_id_type=MESH)
    for n in range(2):
        multiply_a(n, 3)
        multiply_b(n, 3)

    spread()
    zsend[0] = sweep(0)
    pl.semaphore_wait(token, 2)
    sent = list(started)
    started.clear()
    waits = []
    for dz, peer in line:
        copy = remote(zsend.at[0], bbuf.at[dz], peer)
        go(copy)
        waits.append(copy)
    bbuf[0] = zsend[0]
    for copy in sent:
        copy.wait_send()
    for copy in waits:
        copy.wait_recv()
    gsend[...] = own_w - lse2(bbuf[...])
    gbuf[0] = gsend[...]
    waits = []
    place_of, offset_of = (0, 2, 3, 1), (0, 3, 1, 2)
    for p in range(7, 0, -1):
        out, dy = p // 4, offset_of[p % 4]
        there = out * 4 + place_of[(4 - dy) % 4]
        copy = remote(gsend, gbuf.at[there], at(out, dy, 0, core))
        go(copy)
        waits.append((there, count[0] - 1))
    for there, slot in waits:
        remote(gbuf.at[there], gbuf.at[there], partner, slot).wait_recv()

    spread()
    zsend[1] = sweep(1)
    waits = []
    for dz, peer in line:
        copy = remote(zsend.at[1], fbuf.at[0, dz], peer)
        go(copy)
        waits.append(copy)
    for dz, peer in across:
        copy = remote(zsend.at[1], fbuf.at[1, dz], peer)
        go(copy)
        waits.append(copy)
    fbuf[0, 0] = zsend[1]
    row_out[...] = frow[0] * (1.0 / TO2)
    for copy in waits:
        copy.wait_recv()
    hbuf[core] = lse2(fbuf[0])
    hbuf[1 - core] = lse2(fbuf[1])
    total = jnp.zeros((1, 128), jnp.float32)
    within = lax.rem(lanes, 64)
    for c in range(2):
        first, second = hbuf[c, 0:1, :], hbuf[c, 1:2, :]
        out = jnp.zeros((1, 128), jnp.float32)
        for k in range(4):
            w = jnp.where(
                within < 32,
                pltpu.roll(first, (64 * c - 32 * k) % 128, 1),
                pltpu.roll(second, (64 * c + 32 - 32 * k) % 128, 1),
            )
            out = jnp.where(zl == k, w, out)
        total = jnp.where(lax.div(lanes, 64) == c, out, total)
    col_out[...] = 0.1 * tlogw_in[...] - (1.0 / TO2) * total

    for copy in started:
        copy.wait_send()


N_SEM = 66 + 9 + 12 + 12 + 16 + 7 + 7 + 15


def shards(source_embed, target_embed, target_init, source_logw, target_logw):
    f32, bf16 = jnp.float32, jnp.bfloat16
    vmem = pl.BlockSpec(memory_space=pltpu.VMEM)
    hbm = pl.BlockSpec(memory_space=pl.ANY)
    row, col = pl.pallas_call(
        kernel,
        out_shape=(jax.ShapeDtypeStruct((4, 128), f32), jax.ShapeDtypeStruct((1, 128), f32)),
        in_specs=[hbm, hbm, vmem, vmem, vmem],
        out_specs=(vmem, vmem),
        scratch_shapes=[
            pltpu.VMEM((2048, D), bf16),
            pltpu.VMEM((R, R, 2, 32, D), bf16),
            pltpu.VMEM((R, R, 2, 32, D), bf16),
            pltpu.VMEM((R, R, 2, 2, 128), f32),
            pltpu.VMEM((16, 2048, 128), f32),
            pltpu.VMEM((16, 8, 128), f32),
            pltpu.VMEM((2, 128), f32),
            pltpu.VMEM((8, 2, 128), f32),
            pltpu.VMEM((2048, 128), f32),
            pltpu.VMEM((2048, 128), f32),
            pltpu.VMEM((2048, 128), f32),
            pltpu.VMEM((4, 4, 128), f32),
            pltpu.VMEM((4, 4, 128), f32),
            pltpu.VMEM((2, 3, 4, 4, 128), f32),
            pltpu.VMEM((4, 4, 128), f32),
            pltpu.VMEM((16, 8, 128), f32),
            pltpu.VMEM((16, 8, 128), f32),
            pltpu.VMEM((8, 1, 128), f32),
            pltpu.VMEM((8, 2, 128), f32),
            pltpu.VMEM((2, 8, 2, 128), f32),
            pltpu.VMEM((2, 2, 128), f32),
            pltpu.VMEM((8, 2, 128), f32),
            pltpu.VMEM((2, 8, 2, 128), f32),
            pltpu.VMEM((2, 2, 128), f32),
            pltpu.SemaphoreType.DMA((N_SEM,)),
            pltpu.SemaphoreType.DMA((N_SEM,)),
            pltpu.SemaphoreType.DMA((4,)),
            pltpu.SemaphoreType.REGULAR,
        ],
        compiler_params=pltpu.CompilerParams(
            collective_id=0, has_side_effects=True, vmem_limit_bytes=60 * 2**20
        ),
    )(
        source_embed, target_embed, target_init.reshape(1, 128),
        source_logw.reshape(4, 128), target_logw.reshape(1, 128),
    )
    return row.reshape(512), col.reshape(128)


def solution(mesh):
    in_specs = (P(("blk", "grp"), None), P("blk", None), P("blk"), P(("blk", "grp")), P("blk"))
    out_specs = (P(("blk", "grp")), P("blk"))
    return jax.shard_map(shards, mesh=mesh, in_specs=in_specs, out_specs=out_specs, check_vma=False)
```

```python
import math

import jax
import jax.numpy as jnp
from jax import lax
from jax.experimental import pallas as pl
from jax.experimental.pallas import tpu as pltpu
from jax.sharding import PartitionSpec as P

D = 768
LOG2E = math.log2(math.e)
TO2 = 10.0 * LOG2E
SCALE = TO2 / math.sqrt(D)
NZ = 8
R = 4
MESH = pl.DeviceIdType.MESH


def lse2(stack):
    top = jnp.max(stack, axis=0)
    return top + jnp.log2(jnp.sum(jnp.exp2(stack - top[None]), axis=0))


def rem4(v):
    return lax.rem(v, 4)


def kernel(
    src_in, tgt_in, init_in, slogw_in, tlogw_in, row_out, col_out,
    src, buf_a, buf_b, aux, cost, grep, gsend, gbuf, mrow, srow, frep, wrow, lrow, lget, frow,
    ctop, csum, ltile, lsend, abuf, zsend, bbuf, fbuf, hbuf,
    send, recv, loc, token,
):
    b, g = lax.axis_index("blk"), lax.axis_index("grp")
    core, zh = lax.rem(g, 2), lax.div(g, 2)
    zl, x, y = lax.div(b, 16), rem4(lax.div(b, 4)), rem4(b)
    z = zh * 4 + zl
    x_in, x_out = x + 1 - 2 * lax.rem(x, 2), 3 - x

    def dev(px, py, pz, pc):
        return (rem4(pz) * 16 + px * 4 + py, lax.div(pz, 4) * 2 + pc)

    def at(out, dy, dz, pc):
        px = jnp.where(out == 1, x_out, x)
        return dev(px, rem4(y + dy + 4), lax.rem(z + dz + NZ, NZ), pc)

    def step(dim, by):
        return at(0, by if dim == "y" else 0, by if dim == "z" else 0, core)

    partner = at(0, 0, 0, 1 - core)
    mates = [partner, dev(x_in, y, z, core), dev(x_in, y, z, 1 - core)]
    opposite = at(1, 0, 0, core)
    line = [(dz, at(0, 0, dz, core)) for dz in range(1, NZ)]
    across = [(dz, at(0, 0, dz, 1 - core)) for dz in range(NZ)]

    barrier = pltpu.get_barrier_semaphore()
    peers = [step(d, by) for d in ("y", "z") for by in (1, -1)] + mates + [opposite]
    for peer in peers:
        pl.semaphore_signal(barrier, inc=1, device_id=peer, device_id_type=MESH)

    half = pl.multiple_of(core * 64, 64)
    locals_ = [
        pltpu.make_async_copy(tgt_in.at[pl.ds(half, 32), :], buf_a.at[0, 0, 0], loc.at[0]),
        pltpu.make_async_copy(tgt_in.at[pl.ds(half + 32, 32), :], buf_b.at[0, 0, 0], loc.at[1]),
        pltpu.make_async_copy(src_in, src.at[pl.ds(0, 512), :], loc.at[2]),
    ]
    for copy in locals_:
        copy.start()
    aux[0, 0, 0] = jnp.concatenate([init_in[...], tlogw_in[...]], axis=0)
    wrow[0] = slogw_in[...]

    count = [0]
    started = []

    def remote(src_ref, dst_ref, to, slot=None):
        if slot is None:
            slot = count[0]
            count[0] += 1
        return pltpu.make_async_remote_copy(
            src_ref=src_ref, dst_ref=dst_ref, send_sem=send.at[slot], recv_sem=recv.at[slot],
            device_id=to, device_id_type=MESH,
        )

    def go(copy):
        copy.start()
        started.append(copy)

    def drop(copy):
        started[:] = [c for c in started if c is not copy]

    class Ring:
        def __init__(self, dim, unit, low=None, high=None):
            self.dim, self.unit = dim, unit
            self.low, self.high = low or unit, high
            self.base = count[0]
            count[0] += 4
            self.up, self.down = step(dim, 1), step(dim, -1)

        def begin(self):
            go(remote(self.unit(0), self.unit(1), self.up, self.base))
            go(remote(self.unit(0), self.unit(2), self.down, self.base + 1))

        def mid(self):
            remote(self.unit(1), self.unit(1), self.up, self.base).wait_recv()
            go(remote(self.low(1), self.low(3), self.up, self.base + 2))
            remote(self.unit(2), self.unit(2), self.down, self.base + 1).wait_recv()
            if self.high is not None:
                go(remote(self.high(2), self.high(3), self.down, self.base + 3))

        def end(self):
            remote(self.low(3), self.low(3), self.up, self.base + 2).wait_recv()
            if self.high is not None:
                remote(self.high(3), self.high(3), self.down, self.base + 3).wait_recv()

    class Tree:
        def __init__(self, buf, d1, d2):
            top, end = pl.ds(0, 16), pl.ds(16, 16)
            self.first = remote(buf.at[0, 0, 0], buf.at[0, 0, 1], opposite)

            def single(dim, place):
                return Ring(
                    dim, lambda p: buf.at[place(p)], lambda p: buf.at[place(p) + (top,)], lambda p: buf.at[place(p) + (end,)]
                )

            self.two = [single(d1, lambda p, k=k: (0, p, k)) for k in range(2)]
            self.own = [single(d2, lambda p, k=k: (p, 0, k)) for k in range(2)]
            self.near = [
                Ring(d2, lambda p, k=k: buf.at[p, pl.ds(1, 2), k], lambda p, k=k: buf.at[p, 1, k], lambda p, k=k: buf.at[p, 2, k])
                for k in range(2)
            ]
            self.far = [single(d2, lambda p, k=k: (p, 3, k)) for k in range(2)]

    trees = [Tree(buf_a, "z", "y"), Tree(buf_b, "y", "z")]
    aux_first = remote(aux.at[0, 0, 0], aux.at[0, 0, 1], opposite)
    aux_rings = [Ring("y", lambda p: aux.at[0, p]), Ring("z", lambda p: aux.at[p])]

    def rows(slot, k):
        return src.at[pl.ds(512 * slot + 128 * k, 128), :]

    to_mate = [remote(rows(0, k), rows(2, k), mates[1]) for k in range(4)]
    to_partner = remote(src.at[pl.ds(0, 512), :], src.at[pl.ds(512, 512), :], partner)
    relay = [remote(rows(2, k), rows(3, k), partner) for k in range(4)]
    to_all = [remote(wrow.at[0], wrow.at[k + 1], mates[k]) for k in range(3)]

    for copy in locals_[:2]:
        copy.wait()
    pl.semaphore_wait(barrier, len(peers))

    for t in trees:
        go(t.first)
        t.two[0].begin()
        t.own[0].begin()
    go(aux_first)
    locals_[2].wait()
    for copy in to_mate:
        go(copy)
    go(to_partner)
    for copy in to_all:
        go(copy)

    for t in trees:
        t.first.wait_recv()
        t.two[1].begin()
        t.own[1].begin()
    aux_first.wait_recv()
    aux_rings[0].begin()
    for t in trees:
        t.two[0].mid()
        t.near[0].begin()
    aux_rings[0].mid()
    for t in trees:
        t.own[0].mid()
    for t in trees:
        t.two[1].mid()
        t.near[1].begin()
    for t in trees:
        t.own[1].mid()
    aux_rings[0].end()
    aux_rings[1].begin()
    for t in trees:
        t.two[0].end()
        t.far[0].begin()
    to_mate[0].wait_recv()
    go(relay[0])
    for t in trees:
        t.two[1].end()
        t.far[1].begin()
    aux_rings[1].mid()
    for copy in to_all:
        copy.wait_recv()
    to_partner.wait_recv()

    zplace = []
    for k in range(4):
        r = rem4(k - zl + 4)
        zplace.append(jnp.where(r == 0, 0, jnp.where(r == 3, 1, jnp.where(r == 1, 2, 3))))

    def multiply(h, pieces, tiles):
        r = slice(1024 * h, 1024 * h + 1024)
        out = SCALE * lax.dot_general(
            src[r, :], jnp.concatenate(pieces, axis=0), (((1,), (1,)), ((), ())), preferred_element_type=jnp.float32
        )
        cost[tiles[0], r, :] = out[:, :128]
        cost[tiles[1], r, :] = out[:, 128:]

    def multiply_a(h, pv):
        multiply(h, [buf_a[pv, zp, k] for k in range(2) for zp in zplace], (pv, 4 + pv))

    def multiply_b(h, pz):
        multiply(h, [buf_b[pz, pv, k] for k in range(2) for pv in range(4)], (8 + 2 * pz, 9 + 2 * pz))

    for t in trees:
        t.near[0].mid()
    multiply_a(0, 0)
    for t in trees:
        t.near[1].mid()
    to_mate[1].wait_recv()
    go(relay[1])
    multiply_b(0, 0)
    for k in range(2):
        for t in trees:
            t.far[k].mid()
    aux_rings[1].end()
    to_mate[2].wait_recv()
    go(relay[2])

    @pl.loop(1, 3)
    def _(i):
        multiply_a(0, i)
        multiply_b(0, i)

    to_mate[3].wait_recv()
    go(relay[3])

    lanes = lax.broadcasted_iota(jnp.int32, (1, 128), 1)
    low_half = lanes < 64
    chunk = lax.div(lanes, 32)

    def group_of(blocks):
        first = second = jnp.zeros((1, 128), jnp.float32)
        for k, block in enumerate(blocks):
            w = jnp.where(core == 0, block, pltpu.roll(block, 64, 1))
            first = jnp.where(chunk == k, pltpu.roll(w, (k * 32) % 128, 1), first)
            second = jnp.where(chunk == k, pltpu.roll(w, (k * 32 - 32) % 128, 1), second)
        return jnp.concatenate([first, second], axis=0)

    for k in range(2):
        for pv in range(4):
            gbuf[k * 4 + pv] = TO2 * group_of([aux[zp, pv, k, 0:1, :] for zp in zplace])
    own_w = LOG2E * group_of([aux[zp, 0, 0, 1:2, :] for zp in zplace])

    eye = lax.broadcasted_iota(jnp.int32, (128, 128), 0) == lax.broadcasted_iota(jnp.int32, (128, 128), 1)

    def spread():
        for p in range(8):
            grep[p] = jnp.broadcast_to(gbuf[p, 0:1, :], (8, 128))
        for n, zp in enumerate(zplace):
            for k in range(2):
                tile = jnp.zeros((1, 128), jnp.float32)
                for pv in range(4):
                    w = pltpu.roll(gbuf[k * 4 + pv, 1:2, :], (32 * pv - 32 * n) % 128, 1)
                    tile = jnp.where(chunk == pv, w, tile)
                grep[8 + zp * 2 + k] = jnp.broadcast_to(tile, (8, 128))

    halves = [lax.rem(x + k, 2) for k in range(2)]

    def row_pass(hd):
        @pl.loop(0, 128, unroll=8)
        def _(i):
            r = pl.ds(pl.multiple_of(1024 * hd + i * 8, 8), 8)
            top = total = None
            for c in range(0, 16, 8):
                stack = jnp.stack([cost[t, r, :] + grep[t] for t in range(c, c + 8)])
                new = jnp.max(stack, axis=0)
                if top is not None:
                    new = jnp.maximum(top, new)
                part = jnp.sum(jnp.exp2(stack - new[None]), axis=0)
                total = part if top is None else total * jnp.exp2(top - new) + part
                top = new
            mrow[r, :] = top
            srow[r, :] = total

        for k in range(2):
            for q in range(4):
                r = pl.ds(pl.multiple_of(1024 * hd + 512 * k + 128 * q, 128), 128)
                m = mrow[r, :].T
                top = jnp.max(m, axis=0, keepdims=True)
                total = jnp.sum(srow[r, :].T * jnp.exp2(m - top), axis=0, keepdims=True)
                lrow[2 * hd + k, q : q + 1, :] = top + jnp.log2(total)

    def swap_rows(it, hd):
        swaps = []
        for k in range(3):
            theirs = hd if k == 0 else 1 - hd
            mine = pl.ds(2 * hd, 2)
            copy = remote(lrow.at[mine], lget.at[it, k, mine], mates[k])
            copy.start()
            other = lget.at[it, k, pl.ds(2 * theirs, 2)]
            swaps.append((copy, remote(other, other, mates[k], count[0] - 1)))
        return swaps

    def finish_rows(it, hd, swaps):
        for copy, arrival in swaps:
            arrival.wait_recv()
            copy.wait_send()
        for k in range(2):
            slot = 2 * hd + k
            terms = [
                lrow[slot], lget[it, 0, 2 * hd + 1 - k], lget[it, 1, 2 * (1 - hd) + k], lget[it, 2, 2 * (1 - hd) + 1 - k],
            ]
            frow[slot] = LOG2E * wrow[slot] - lse2(jnp.stack(terms))
            for q in range(4):
                r = pl.ds(pl.multiple_of(1024 * hd + 512 * k + 128 * q, 128), 128)
                line_ = jnp.broadcast_to(frow[slot, q : q + 1, :], (128, 128))
                col = jnp.sum(jnp.where(eye, line_, 0.0), axis=1, keepdims=True)
                frep[r, :] = jnp.broadcast_to(col, (128, 128))

    def sweep(it):
        row_pass(halves[0])
        early = swap_rows(it, halves[0])
        row_pass(halves[1])
        late = swap_rows(it, halves[1])
        finish_rows(it, halves[0], early)

        @pl.loop(0, 16, unroll=2)
        def _(t):
            ctop[t], csum[t] = col_half(t, halves[0], None, None)

        finish_rows(it, halves[1], late)
        return col_reduce(it)

    def offset(place):
        return jnp.where(place == 0, 0, jnp.where(place == 1, 3, jnp.where(place == 2, 1, 2)))

    def col_half(tile, hd, top, total):
        for q in range(8):
            r = pl.ds(pl.multiple_of(1024 * hd + 128 * q, 128), 128)
            w = (cost[tile, r, :] + frep[r, :]).reshape(16, 8, 128)
            new = jnp.max(w, axis=0)
            if top is not None:
                new = jnp.maximum(top, new)
            part = jnp.sum(jnp.exp2(w - new[None]), axis=0)
            total = part if top is None else total * jnp.exp2(top - new) + part
            top = new
        return top, total

    def col_tile(tile):
        top, total = col_half(tile, halves[1], ctop[tile], csum[tile])
        peak = jnp.max(top, axis=0, keepdims=True)
        mass = jnp.sum(total * jnp.exp2(top - peak), axis=0, keepdims=True)
        return peak + jnp.log2(mass)

    def col_reduce(it):
        base = count[0]
        count[0] += 8

        def give(p):
            to = at(lax.div(p, 4), offset(rem4(p)), 0, core)
            return remote(lsend.at[p], abuf.at[it, p], to, base + p)

        def group(i):
            return (1 - lax.rem(i, 2)) * 4 + 3 - lax.div(i, 2)

        @pl.loop(0, 8, unroll=2)
        def _(i):
            ltile[i] = col_tile(8 + i)

        for k in range(2):
            for pv in range(4):
                line_ = jnp.zeros((1, 128), jnp.float32)
                for n, zp in enumerate(zplace):
                    w = pltpu.roll(ltile[zp * 2 + k], (32 * n - 32 * pv) % 128, 1)
                    line_ = jnp.where(chunk == n, w, line_)
                lsend[k * 4 + pv, 1:2, :] = line_

        @pl.loop(0, 8)
        def _(i):
            p = group(i)
            lsend[p, 0:1, :] = col_tile(p)

            @pl.when(i > 0)
            def _():
                give(group(i - 1)).start()

        abuf[it, 0] = lsend[0]

        @pl.loop(1, 8)
        def _(p):
            copy = give(p)
            copy.wait_recv()
            copy.wait_send()

        return lse2(abuf[it])

    for copy in relay:
        copy.wait_recv()

    @pl.loop(0, 3)
    def _(i):
        multiply_a(1, i)
        multiply_b(1, i)

    for t in trees:
        for ring in t.own + t.near + t.far:
            ring.end()
    for by in (2, -2):
        pl.semaphore_signal(token, inc=1, device_id=step("z", by), device_id_type=MESH)
    for n in range(2):
        multiply_a(n, 3)
        multiply_b(n, 3)

    spread()
    zsend[0] = sweep(0)
    pl.semaphore_wait(token, 2)
    sent = list(started)
    started.clear()
    waits = []
    for dz, peer in line:
        copy = remote(zsend.at[0], bbuf.at[dz], peer)
        go(copy)
        waits.append(copy)
    bbuf[0] = zsend[0]
    for copy in sent:
        copy.wait_send()
    for copy in waits:
        copy.wait_recv()
    gsend[...] = own_w - lse2(bbuf[...])
    gbuf[0] = gsend[...]
    waits = []
    place_of, offset_of = (0, 2, 3, 1), (0, 3, 1, 2)
    for p in range(7, 0, -1):
        out, dy = p // 4, offset_of[p % 4]
        there = out * 4 + place_of[(4 - dy) % 4]
        copy = remote(gsend, gbuf.at[there], at(out, dy, 0, core))
        go(copy)
        waits.append((there, count[0] - 1))
    for there, slot in waits:
        remote(gbuf.at[there], gbuf.at[there], partner, slot).wait_recv()

    spread()
    zsend[1] = sweep(1)
    waits = []
    for dz, peer in line:
        copy = remote(zsend.at[1], fbuf.at[0, dz], peer)
        go(copy)
        waits.append(copy)
    for dz, peer in across:
        copy = remote(zsend.at[1], fbuf.at[1, dz], peer)
        go(copy)
        waits.append(copy)
    fbuf[0, 0] = zsend[1]
    for q in range(4):
        row_out[128 * q : 128 * q + 128] = frow[0, q] * (1.0 / TO2)
    for copy in waits:
        copy.wait_recv()
    hbuf[core] = lse2(fbuf[0])
    hbuf[1 - core] = lse2(fbuf[1])
    total = jnp.zeros((1, 128), jnp.float32)
    within = lax.rem(lanes, 64)
    for c in range(2):
        first, second = hbuf[c, 0:1, :], hbuf[c, 1:2, :]
        out = jnp.zeros((1, 128), jnp.float32)
        for k in range(4):
            w = jnp.where(
                within < 32,
                pltpu.roll(first, (64 * c - 32 * k) % 128, 1),
                pltpu.roll(second, (64 * c + 32 - 32 * k) % 128, 1),
            )
            out = jnp.where(zl == k, w, out)
        total = jnp.where(lax.div(lanes, 64) == c, out, total)
    col_out[...] = (0.1 * tlogw_in[...] - (1.0 / TO2) * total)[0]

    for copy in started:
        copy.wait_send()


N_SEM = 66 + 9 + 12 + 12 + 16 + 7 + 7 + 15


def shards(source_embed, target_embed, target_init, source_logw, target_logw):
    f32, bf16 = jnp.float32, jnp.bfloat16
    vmem = pl.BlockSpec(memory_space=pltpu.VMEM)
    hbm = pl.BlockSpec(memory_space=pl.ANY)
    row, col = pl.pallas_call(
        kernel,
        out_shape=(jax.ShapeDtypeStruct((512,), f32), jax.ShapeDtypeStruct((128,), f32)),
        in_specs=[hbm, hbm, vmem, vmem, vmem],
        out_specs=(vmem, vmem),
        scratch_shapes=[
            pltpu.VMEM((2048, D), bf16),
            pltpu.VMEM((R, R, 2, 32, D), bf16),
            pltpu.VMEM((R, R, 2, 32, D), bf16),
            pltpu.VMEM((R, R, 2, 2, 128), f32),
            pltpu.VMEM((16, 2048, 128), f32),
            pltpu.VMEM((16, 8, 128), f32),
            pltpu.VMEM((2, 128), f32),
            pltpu.VMEM((8, 2, 128), f32),
            pltpu.VMEM((2048, 128), f32),
            pltpu.VMEM((2048, 128), f32),
            pltpu.VMEM((2048, 128), f32),
            pltpu.VMEM((4, 4, 128), f32),
            pltpu.VMEM((4, 4, 128), f32),
            pltpu.VMEM((2, 3, 4, 4, 128), f32),
            pltpu.VMEM((4, 4, 128), f32),
            pltpu.VMEM((16, 8, 128), f32),
            pltpu.VMEM((16, 8, 128), f32),
            pltpu.VMEM((8, 1, 128), f32),
            pltpu.VMEM((8, 2, 128), f32),
            pltpu.VMEM((2, 8, 2, 128), f32),
            pltpu.VMEM((2, 2, 128), f32),
            pltpu.VMEM((8, 2, 128), f32),
            pltpu.VMEM((2, 8, 2, 128), f32),
            pltpu.VMEM((2, 2, 128), f32),
            pltpu.SemaphoreType.DMA((N_SEM,)),
            pltpu.SemaphoreType.DMA((N_SEM,)),
            pltpu.SemaphoreType.DMA((4,)),
            pltpu.SemaphoreType.REGULAR,
        ],
        compiler_params=pltpu.CompilerParams(
            collective_id=0, has_side_effects=True, vmem_limit_bytes=60 * 2**20
        ),
    )(
        source_embed, target_embed, target_init.reshape(1, 128),
        source_logw.reshape(4, 128), target_logw.reshape(1, 128),
    )
    return row, col


def solution(mesh):
    in_specs = (P(("blk", "grp"), None), P("blk", None), P("blk"), P(("blk", "grp")), P("blk"))
    out_specs = (P(("blk", "grp")), P("blk"))
    return jax.shard_map(shards, mesh=mesh, in_specs=in_specs, out_specs=out_specs, check_vma=False)
```
